32 devices in a mesh: gy: 8 (over z, x), gz: 4 (over y, core).
Axes of the slice: x: 2, y: 2, z: 4, core: 2. Of those that a mesh axis runs over, the one named last changes fastest.
Arguments:
- tokens: bfloat16 [16, 64, 16, 192], P(None, 'gy', 'gz'), may hold values from -36 to 36
- qkv_weight: bfloat16 [192, 576], replicated, may hold values from -0.4375 to 0.4375
- out_weight: bfloat16 [192, 192], replicated, may hold values from -1.25 to 1.25
- conv_kernel: float32 [3, 3, 3, 192], replicated, may hold values from -1.25 to 1.25
- up_weight: bfloat16 [192, 768], replicated, may hold values from -0.4375 to 0.4375
- down_weight: bfloat16 [768, 192], replicated, may hold values from -0.21875 to 0.21875
- band_mask: int32 [4, 4], replicated, may hold values from 0 to 1, as said below
- grad_out: bfloat16 [16, 64, 16, 192], P(None, 'gy', 'gz'), may hold values from -6 to 6
Outputs:
- block_out: bfloat16 [16, 64, 16, 192], P(None, 'gy', 'gz')
- token_gradient: bfloat16 [16, 64, 16, 192], P(None, 'gy', 'gz')
- qkv_gradient: float32 [192, 576], replicated
- out_gradient: float32 [192, 192], replicated
- kernel_gradient: float32 [3, 3, 3, 192], replicated
- up_gradient: float32 [192, 768], replicated
- down_gradient: float32 [768, 192], replicated
The draws below stay inside these ranges and needn't reach their ends.
Inputs may be any that keep to these rules, and one draw needn't show every extreme that they name: band_mask[i, i] is 1, and band_mask[i, j] is 0 where |i - j| > 4; other entries are 0 or 1.
All inputs are finite; a program needn't handle non-finite values.
Results may differ from the reference program's by a relative error of at most 0.017.
Values may be sent and summed in bfloat16 or wider, within the bound.
A program may use at most 64 MiB of HBM per device.

```python
import math
import jax
import jax.numpy as jnp
from jax import lax

C = 192
HEADS = 6
F = 768
BLOCK = 16
BAND = 4
X = 16
Y = 64
Z = 16
NBY = 4


def draw_tokens(key, part):
    noise_key, row_key, column_key = jax.random.split(key, 3)
    column_scale = jnp.exp(jax.random.uniform(column_key, (C,), jnp.float32, math.log(0.3), math.log(3.0)))
    noise_field = jax.random.truncated_normal(noise_key, -4.0, 4.0, (X, Y, Z, C), jnp.float32)
    row_scale = jnp.exp(jax.random.uniform(row_key, (X, Y, Z, 1), jnp.float32, math.log(0.3), math.log(3.0)))
    token_field = noise_field * row_scale * column_scale
    return token_field.astype(jnp.bfloat16)


def draw_band_mask(key, part):
    rows_index = jnp.arange(NBY, dtype=jnp.int32)[:, None]
    cols_index = jnp.arange(NBY, dtype=jnp.int32)[None, :]
    distance = jnp.abs(rows_index - cols_index)
    coin_flips = jax.random.randint(key, (NBY, NBY), 0, 4, dtype=jnp.int32)
    kept_blocks = jnp.where(coin_flips > 0, 1, 0)
    return jnp.where(distance == 0, 1, jnp.where(distance <= BAND, kept_blocks, 0)).astype(jnp.int32)


def shard_levels(key, shape, cuts, smallest, largest):
    loudness = 1.0
    for position, parts in cuts:
        draws = jax.random.uniform(jax.random.fold_in(jax.random.fold_in(key, 6), position), (parts,), jnp.float32, smallest / len(cuts), largest / len(cuts))
        loudness = loudness * jnp.repeat(jnp.exp(draws), shape[position] // parts).reshape((-1,) + (1,) * (len(shape) - 1 - position))
    return loudness


def bell_draw(key, shape, spread, most, cuts=(), kind=jnp.bfloat16):
    loudness = shard_levels(key, shape, cuts, -0.22, 0.18) if cuts else 1.0
    result = jax.random.normal(key, shape, jnp.float32) * spread * loudness
    return jnp.minimum(jnp.maximum(result, -most), most).astype(kind)


def setup_inputs(seed: int = 0) -> dict:
    key_list = jax.random.split(jax.random.key(seed), 9)
    return {
        "tokens": draw_tokens(jax.random.fold_in(key_list[8], 71), 0),
        "qkv_weight": bell_draw(key_list[1], (C, 3 * C), C ** -0.5, 0.4375),
        "out_weight": bell_draw(key_list[2], (C, C), (C // 8) ** -0.5, 1.25),
        "conv_kernel": bell_draw(key_list[3], (3, 3, 3, C), 27 ** -0.5, 1.25, (), jnp.float32),
        "up_weight": bell_draw(key_list[4], (C, F), C ** -0.5, 0.4375),
        "down_weight": bell_draw(key_list[5], (F, C), F ** -0.5, 0.21875),
        "band_mask": draw_band_mask(jax.random.fold_in(key_list[8], 71), 0),
        "grad_out": bell_draw(key_list[7], (X, Y, Z, C), 1.0, 6.0, ((1, 8), (2, 4))),
    }


NORM_EPS = 1e-05
UNIT_EPS = 1e-06
GELU_SLOPE = 0.7978845608028654
GELU_CUBIC = 0.044715

def norm_rows(values):
    centred = values - lax.optimization_barrier(jnp.mean(values, axis=-1, keepdims=True))
    inverse = lax.rsqrt(lax.optimization_barrier(jnp.mean(centred * centred, axis=-1, keepdims=True)) + NORM_EPS)
    return (centred * inverse, inverse)

def norm_rows_back(upstream, normal, inverse):
    return inverse * (upstream - lax.optimization_barrier(jnp.mean(upstream, axis=-1, keepdims=True)) - normal * lax.optimization_barrier(jnp.mean(upstream * normal, axis=-1, keepdims=True)))

def unit_scale(values):
    return lax.rsqrt(lax.optimization_barrier(jnp.mean(values * values, axis=-1, keepdims=True)) + UNIT_EPS)

def unit_back(upstream, values, scaling):
    return scaling * upstream - scaling * scaling * scaling * values * lax.optimization_barrier(jnp.mean(upstream * values, axis=-1, keepdims=True))

def gelu_value(pre_act):
    return 0.5 * pre_act * (1.0 + jnp.tanh(GELU_SLOPE * (pre_act + GELU_CUBIC * pre_act * pre_act * pre_act)))

def gelu_slope(pre_act):
    tangent = jnp.tanh(GELU_SLOPE * (pre_act + GELU_CUBIC * pre_act * pre_act * pre_act))
    return 0.5 * (1.0 + tangent) + 0.5 * pre_act * (1.0 - tangent * tangent) * GELU_SLOPE * (1.0 + 3.0 * GELU_CUBIC * pre_act * pre_act)

def flatten_rows(values):
    return values.reshape(-1, values.shape[-1])

def project(values, weight):
    summed = jnp.dot(flatten_rows(values), weight, preferred_element_type=jnp.float32)
    return summed.reshape(values.shape[:-1] + (weight.shape[1],))

def project_back(values, weight):
    summed = lax.dot_general(flatten_rows(values), weight, (((1,), (1,)), ((), ())), preferred_element_type=jnp.float32)
    return summed.reshape(values.shape[:-1] + (weight.shape[0],))

def contract(left_rows, right_rows):
    return lax.dot_general(flatten_rows(left_rows), flatten_rows(right_rows), (((0,), (0,)), ((), ())), preferred_element_type=jnp.float32)

def split_heads(values, head_count):
    return values.reshape(values.shape[:-1] + (head_count, values.shape[-1] // head_count))

def join_heads(values):
    return values.reshape(values.shape[:-2] + (values.shape[-2] * values.shape[-1],))

def head_product(einsum_form, left_side, right_side):
    return jnp.einsum(einsum_form, left_side.astype(jnp.float32), right_side.astype(jnp.float32))

def attention_parts(qkv_rows, mask_full, head_count):
    feature_width = qkv_rows.shape[-1] // 3
    query_vec = qkv_rows[..., :feature_width].astype(jnp.float32)
    key_vec = qkv_rows[..., feature_width:2 * feature_width].astype(jnp.float32)
    query_scale = unit_scale(query_vec)
    key_scale = unit_scale(key_vec)
    query_unit = (query_vec * query_scale).astype(jnp.bfloat16)
    key_unit = (key_vec * key_scale).astype(jnp.bfloat16)
    factor = 2.0 / math.sqrt(feature_width // head_count)
    scores = head_product('aibhd,ajbhd->abhij', split_heads(query_unit, head_count), split_heads(key_unit, head_count))
    weights = mask_full * jnp.exp(factor * scores)
    attn_probs = weights / lax.optimization_barrier(jnp.sum(weights, axis=-1, keepdims=True))
    return (query_vec, key_vec, query_scale, key_scale, query_unit, key_unit, attn_probs, factor)

def attend(qkv_rows, mask_full, head_count):
    query_vec, key_vec, query_scale, key_scale, query_unit, key_unit, attn_probs, factor = attention_parts(qkv_rows, mask_full, head_count)
    feature_width = qkv_rows.shape[-1] // 3
    value_heads = split_heads(qkv_rows[..., 2 * feature_width:], head_count)
    probs_low = attn_probs.astype(jnp.bfloat16)
    mixed_heads = head_product('abhij,ajbhd->aibhd', probs_low, value_heads)
    return join_heads(mixed_heads).astype(jnp.bfloat16)

def attend_back(qkv_rows, mask_full, head_count, upstream):
    query_vec, key_vec, query_scale, key_scale, query_unit, key_unit, attn_probs, factor = attention_parts(qkv_rows, mask_full, head_count)
    feature_width = qkv_rows.shape[-1] // 3
    value_heads = split_heads(qkv_rows[..., 2 * feature_width:], head_count)
    grad_heads = split_heads(upstream, head_count)
    probs_low = attn_probs.astype(jnp.bfloat16)
    grad_probs = head_product('aibhd,ajbhd->abhij', grad_heads, value_heads)
    grad_values = head_product('abhij,aibhd->ajbhd', probs_low, grad_heads)
    grad_scores = attn_probs * (grad_probs - lax.optimization_barrier(jnp.sum(grad_probs * attn_probs, axis=-1, keepdims=True)))
    grad_low = (factor * grad_scores).astype(jnp.bfloat16)
    grad_qunit = join_heads(head_product('abhij,ajbhd->aibhd', grad_low, split_heads(key_unit, head_count)))
    grad_kunit = join_heads(head_product('abhij,aibhd->ajbhd', grad_low, split_heads(query_unit, head_count)))
    grad_query = unit_back(grad_qunit, query_vec, query_scale).astype(jnp.bfloat16)
    grad_key = unit_back(grad_kunit, key_vec, key_scale).astype(jnp.bfloat16)
    return jnp.concatenate([grad_query, grad_key, join_heads(grad_values).astype(jnp.bfloat16)], axis=-1)

def conv_apply(padded, kernel_taps):
    extent_x = padded.shape[0] - 2
    extent_y = padded.shape[1] - 2
    extent_z = padded.shape[2] - 2
    summed = jnp.zeros((extent_x, extent_y, extent_z, padded.shape[3]), jnp.float32)
    for shift_x in range(3):
        for shift_y in range(3):
            for shift_z in range(3):
                window = padded[shift_x:shift_x + extent_x, shift_y:shift_y + extent_y, shift_z:shift_z + extent_z]
                summed = summed + kernel_taps[shift_x, shift_y, shift_z] * window.astype(jnp.float32)
    return summed

def kernel_grad(padded, upstream):
    extent_x, extent_y, extent_z, channels = upstream.shape
    upstream_wide = upstream.astype(jnp.float32)
    pieces = []
    for shift_x in range(3):
        for shift_y in range(3):
            for shift_z in range(3):
                window = padded[shift_x:shift_x + extent_x, shift_y:shift_y + extent_y, shift_z:shift_z + extent_z]
                pieces.append(lax.optimization_barrier(jnp.sum(window.astype(jnp.float32) * upstream_wide, axis=(0, 1, 2))))
    return jnp.stack(pieces).reshape(3, 3, 3, channels)

def mlp_pass(mixed_field, upstream, up_weight, down_weight):
    mixed_wide = mixed_field.astype(jnp.float32)
    normal, inverse = norm_rows(mixed_wide)
    normed = normal.astype(jnp.bfloat16)
    pre_act = project(normed, up_weight)
    hidden = gelu_value(pre_act).astype(jnp.bfloat16)
    block_out = (mixed_wide + project(hidden, down_weight)).astype(jnp.bfloat16)
    grad_hidden = project_back(upstream, down_weight).astype(jnp.bfloat16)
    part_down = contract(hidden, upstream)
    grad_pre = (grad_hidden.astype(jnp.float32) * gelu_slope(pre_act)).astype(jnp.bfloat16)
    part_up = contract(normed, grad_pre)
    grad_normed = project_back(grad_pre, up_weight)
    grad_mixed = (upstream.astype(jnp.float32) + norm_rows_back(grad_normed, normal, inverse)).astype(jnp.bfloat16)
    return (block_out, grad_mixed, part_up, part_down)

def pad_box(field_values):
    wrapped = jnp.pad(field_values, ((0, 0), (1, 1), (1, 1), (0, 0)), mode='wrap')
    return jnp.pad(wrapped, ((1, 1), (0, 0), (0, 0), (0, 0)))

def reference(tokens, qkv_weight, out_weight, conv_kernel, up_weight, down_weight, band_mask, grad_out):
    block_count = band_mask.shape[0]
    line_length = block_count * BLOCK
    mask_full = jnp.broadcast_to(band_mask[:, None, :, None], (block_count, BLOCK, block_count, BLOCK)).reshape(line_length, line_length).astype(jnp.float32)
    flipped = conv_kernel[::-1, ::-1, ::-1]

    def forward_slab(token_slab):
        token_wide = token_slab[None].astype(jnp.float32)
        normal, inverse = norm_rows(token_wide)
        normed = normal.astype(jnp.bfloat16)
        qkv_rows = project(normed, qkv_weight).astype(jnp.bfloat16)
        attended = attend(qkv_rows, mask_full, HEADS)
        return (token_wide + project(attended, out_weight)).astype(jnp.bfloat16)[0]
    value_field = lax.map(forward_slab, tokens)
    padded_value = pad_box(value_field)
    channels = tokens.shape[3]

    def mlp_slab(running, plane_index):
        window = lax.dynamic_slice_in_dim(padded_value, plane_index, 3, 0)
        centre = lax.dynamic_slice_in_dim(value_field, plane_index, 1, 0)
        mixed_field = (centre.astype(jnp.float32) + conv_apply(window, conv_kernel)).astype(jnp.bfloat16)
        upstream = lax.dynamic_slice_in_dim(grad_out, plane_index, 1, 0)
        block_out, grad_mixed, part_up, part_down = mlp_pass(mixed_field, upstream, up_weight, down_weight)
        return ((running[0] + part_up, running[1] + part_down), (block_out[0], grad_mixed[0]))
    start_up = jnp.zeros(up_weight.shape, jnp.float32)
    start_down = jnp.zeros(down_weight.shape, jnp.float32)
    plane_list = jnp.arange(X, dtype=jnp.int32)
    sums_mlp, slabs_mlp = lax.scan(mlp_slab, (start_up, start_down), plane_list)
    block_out_all, grad_mixed_all = slabs_mlp
    padded_grad = pad_box(grad_mixed_all)

    def back_slab(running, plane_index):
        grad_window = lax.dynamic_slice_in_dim(padded_grad, plane_index, 3, 0)
        value_window = lax.dynamic_slice_in_dim(padded_value, plane_index, 3, 0)
        grad_centre = lax.dynamic_slice_in_dim(grad_mixed_all, plane_index, 1, 0)
        grad_value = (grad_centre.astype(jnp.float32) + conv_apply(grad_window, flipped)).astype(jnp.bfloat16)
        part_kernel = kernel_grad(value_window, grad_centre)
        token_slab = lax.dynamic_slice_in_dim(tokens, plane_index, 1, 0)
        token_wide = token_slab.astype(jnp.float32)
        normal, inverse = norm_rows(token_wide)
        normed = normal.astype(jnp.bfloat16)
        qkv_rows = project(normed, qkv_weight).astype(jnp.bfloat16)
        attended = attend(qkv_rows, mask_full, HEADS)
        grad_attended = project_back(grad_value, out_weight).astype(jnp.bfloat16)
        part_out = contract(attended, grad_value)
        grad_qkv = attend_back(qkv_rows, mask_full, HEADS, grad_attended)
        grad_normed = project_back(grad_qkv, qkv_weight).astype(jnp.bfloat16)
        part_qkv = contract(normed, grad_qkv)
        grad_token = (grad_value.astype(jnp.float32) + norm_rows_back(grad_normed.astype(jnp.float32), normal, inverse)).astype(jnp.bfloat16)
        return ((running[0] + part_qkv, running[1] + part_out, running[2] + part_kernel), grad_token[0])
    start_qkv = jnp.zeros(qkv_weight.shape, jnp.float32)
    start_out = jnp.zeros(out_weight.shape, jnp.float32)
    start_kernel = jnp.zeros((3, 3, 3, channels), jnp.float32)
    sums_back, token_gradient = lax.scan(back_slab, (start_qkv, start_out, start_kernel), plane_list)
    factor = 1.0 / math.sqrt(X * Y * Z)
    return (block_out_all, token_gradient, sums_back[0] * factor, sums_back[1] * factor, sums_back[2] * factor, sums_mlp[0] * factor, sums_mlp[1] * factor)
```

```python
import functools
import math
import types

import jax
import jax.numpy as jnp
from jax import lax
from jax.experimental import pallas as pl
from jax.experimental.pallas import tpu as pltpu
from jax.sharding import PartitionSpec as P

HEADS = 6
BLOCK = 16


NORM_EPS = 1e-05
UNIT_EPS = 1e-06
GELU_SLOPE = 0.7978845608028654
GELU_CUBIC = 0.044715

MESH = pl.DeviceIdType.MESH
VMEM = pl.BlockSpec(memory_space=pltpu.VMEM)
ANY = pl.BlockSpec(memory_space=pl.ANY)
LOW = jnp.bfloat16
WIDE = jnp.float32


def norm_rows(values):
    centred = values - jnp.mean(values, axis=-1, keepdims=True)
    inverse = lax.rsqrt(jnp.mean(centred * centred, axis=-1, keepdims=True) + NORM_EPS)
    return (centred * inverse, inverse)


def norm_rows_back(upstream, normal, inverse):
    return inverse * (
        upstream
        - jnp.mean(upstream, axis=-1, keepdims=True)
        - normal * jnp.mean(upstream * normal, axis=-1, keepdims=True)
    )


def unit_scale(values):
    return lax.rsqrt(jnp.mean(values * values, axis=-1, keepdims=True) + UNIT_EPS)


def unit_back(upstream, values, scaling):
    return scaling * upstream - scaling * scaling * scaling * values * jnp.mean(
        upstream * values, axis=-1, keepdims=True
    )


def place_of(index):
    return index + (1 - 2 * lax.rem(index, 2)) * lax.rem(index // 2, 2)


def bits_of(count):
    return [1 << level for level in range(count.bit_length() - 1)]


def dot(left, right, left_axis=1, right_axis=0):
    return lax.dot_general(
        left, right, (((left_axis,), (right_axis,)), ((), ())), preferred_element_type=WIDE
    )


def stack_heads(values):
    width = values.shape[1]
    head_of = lax.broadcasted_iota(jnp.int32, (1, width), 1) // (width // HEADS)
    return jnp.concatenate([jnp.where(head_of == h, values, 0.0) for h in range(HEADS)], axis=0)


def unstack_heads(stacked):
    rows, width = stacked.shape[0] // HEADS, stacked.shape[1]
    head_of = lax.broadcasted_iota(jnp.int32, (1, width), 1) // (width // HEADS)
    joined = stacked[:rows]
    for h in range(1, HEADS):
        joined = jnp.where(head_of == h, stacked[h * rows : (h + 1) * rows], joined)
    return joined


def shift_rows(values, step):
    return pltpu.roll(values, step % values.shape[0], 0)


def face(step, extent):
    return {
        0: (pl.ds(0, extent), pl.ds(1, extent)),
        1: (pl.ds(extent - 1, 1), pl.ds(0, 1)),
        -1: (pl.ds(0, 1), pl.ds(extent + 1, 1)),
    }[step]


def conv_line(padded, taps, plane, column, flip):
    by_shift = [None, None, None]
    for a in range(3):
        for d in range(3):
            window = padded[plane + a, column + d].astype(WIDE)
            for b in range(3):
                tap = taps[2 - a, 2 - b, 2 - d : 3 - d] if flip else taps[a, b, d : d + 1]
                term = tap * window
                by_shift[b] = term if by_shift[b] is None else by_shift[b] + term
    return shift_rows(by_shift[0], 1) + by_shift[1] + shift_rows(by_shift[2], -1)


def put_tiles(target, base, matrix):
    rows = matrix.shape[0] // 16
    for column in range(matrix.shape[1] // 128):
        target[base + column * rows : base + (column + 1) * rows] = matrix[
            :, column * 128 : (column + 1) * 128
        ].reshape(rows, 16, 128)


def spread_mask(mask, length):
    blocks = mask.shape[0]
    row = lax.broadcasted_iota(jnp.int32, (length, blocks), 0) // BLOCK
    column = lax.broadcasted_iota(jnp.int32, (length, blocks), 1)
    pick = jnp.where(row == column, 1.0, 0.0).astype(LOW)
    half = dot(pick, mask.astype(WIDE).astype(LOW)).astype(LOW)
    return dot(half, pick, 1, 1)


def block_kernel(plan, *refs):
    r = types.SimpleNamespace(**dict(zip(plan.names, refs)))
    count_y, count_z = plan.count_y, plan.count_z
    planes, part_y, part_z, width = plan.planes, plan.part_y, plan.part_z, plan.width
    lines, length = planes * part_z, part_y * count_y
    count = lines * length
    factor = 2.0 / math.sqrt(width // HEADS)
    me_y, me_z = lax.axis_index("gy"), lax.axis_index("gz")
    me_x = place_of(me_y)

    loads = [
        pltpu.make_async_copy(source, target, r.load_sem.at[index])
        for index, (source, target) in enumerate(
            (
                (r.qkv_in, r.qkv_weight),
                (r.out_in, r.out_weight),
                (r.taps_in, r.taps),
                (r.up_in, r.up_weight),
                (r.down_in, r.down_weight),
            )
        )
    ]
    for copy in loads:
        copy.start()

    steps = [(dx, dz) for dx in (-1, 0, 1) for dz in (-1, 0, 1) if (dx, dz) != (0, 0)]
    bits = bits_of(count_z)
    depth = len(bits)
    values = [lax.rem(me_z // bit, 2) for bit in bits]
    partners = [(me_y, me_z + bit * (1 - 2 * value)) for bit, value in zip(bits, values)]
    line_peers = [(lax.rem(me_y + k, count_y), me_z) for k in range(1, count_y)]
    barrier = pltpu.get_barrier_semaphore()

    def reach(dx, action):
        if dx == 0:
            action()
        elif dx == 1:
            pl.when(me_x < count_y - 1)(action)
        else:
            pl.when(me_x > 0)(action)

    def place(dx, dz):
        return (place_of(me_x + dx), lax.rem(me_z + dz + count_z, count_z))

    def greet(peer):
        pl.semaphore_signal(barrier, inc=1, device_id=peer, device_id_type=MESH)

    for peer in line_peers + partners:
        greet(peer)
    for dx, dz in steps:
        if dz != 0:
            reach(dx, lambda dx=dx, dz=dz: greet(place(dx, dz)))
    common = len(line_peers) + len(partners)
    inner = (me_x > 0) & (me_x < count_y - 1)

    @pl.when(inner)
    def _():
        pl.semaphore_wait(barrier, common + 6)

    @pl.when(jnp.logical_not(inner))
    def _():
        pl.semaphore_wait(barrier, common + 4)

    def swap(source, target, slot, inward):
        copies = []
        for k in range(1, count_y):
            peer = lax.rem(me_y + k, count_y)
            copy = pltpu.make_async_remote_copy(
                src_ref=source.at[place_of(peer) if inward else peer],
                dst_ref=target.at[me_y if inward else me_x],
                send_sem=r.swap_send.at[slot, k],
                recv_sem=r.swap_recv.at[slot, k],
                device_id=(peer, me_z),
                device_id_type=MESH,
            )
            copy.start()
            copies.append(copy)
        return copies

    token_copies = swap(r.token_in, r.token_got, 0, True)
    grad_copies = swap(r.grad_in, r.grad_got, 1, True)
    r.token_got[me_y] = r.token_in[me_x]
    r.grad_got[me_y] = r.grad_in[me_x]

    def to_lines(got, target):
        for p in range(count_y):
            block = got[p].astype(WIDE)
            for line in range(lines):
                x, z = line // part_z, line % part_z
                target[pl.ds(line * length + p * part_y, part_y)] = block[
                    x * part_y : (x + 1) * part_y, z * width : (z + 1) * width
                ]

    def from_lines(source, target):
        for p in range(count_y):
            rows = [
                jnp.concatenate(
                    [
                        source[pl.ds((x * part_z + z) * length + p * part_y, part_y)]
                        for z in range(part_z)
                    ],
                    axis=1,
                )
                for x in range(planes)
            ]
            target[p] = (rows[0] if planes == 1 else jnp.concatenate(rows, axis=0)).astype(LOW)

    def halo(padded, slot):
        copies = []
        for index, (dx, dz) in enumerate(steps):
            from_x, to_x = face(dx, planes)
            from_z, to_z = face(dz, part_z)
            inside_x = pl.ds(from_x.start + 1, from_x.size)
            inside_z = pl.ds(from_z.start + 1, from_z.size)
            copies.append(
                lambda index=index, dx=dx, dz=dz, ix=inside_x, iz=inside_z, tx=to_x, tz=to_z: pltpu.make_async_remote_copy(
                    src_ref=padded.at[ix, iz],
                    dst_ref=padded.at[tx, tz],
                    send_sem=r.halo_send.at[slot, index],
                    recv_sem=r.halo_recv.at[slot, index],
                    device_id=place(dx, dz),
                    device_id_type=MESH,
                )
            )
        for index, (dx, dz) in enumerate(steps):
            reach(dx, lambda index=index: copies[index]().start())
        blank = jnp.zeros((1,) + tuple(padded.shape[1:]), padded.dtype)

        @pl.when(me_x == 0)
        def _():
            padded[0:1] = blank

        @pl.when(me_x == count_y - 1)
        def _():
            padded[planes + 1 : planes + 2] = blank

        def finish():
            for index, (dx, dz) in enumerate(steps):
                reach(dx, lambda index=index: copies[index]().wait_send())
                reach(-dx, lambda index=index: copies[index]().wait_recv())

        return finish

    def send(source, target, chain, slot, peer):
        copy = pltpu.make_async_remote_copy(
            src_ref=source,
            dst_ref=target,
            send_sem=r.chain_send.at[chain, slot],
            recv_sem=r.chain_recv.at[chain, slot],
            device_id=peer,
            device_id_type=MESH,
        )
        copy.start()
        return copy

    def run_chain(chain):
        entry = plan.chains[chain]
        parts, total, sums = (
            (r.early, r.early_total, r.early_sums)
            if entry.early
            else (r.late, r.late_total, r.late_sums)
        )
        base, size = entry.base, entry.size
        mine = [getattr(r, name) for name in entry.buffers]
        outgoing, incoming = mine[: depth + 1], mine[depth + 1 :]
        held, bases = parts, []
        for level in range(depth):
            half = size // 2
            keep = base + values[level] * half
            away = base + (1 - values[level]) * half
            outgoing[level][...] = held[pl.ds(away, half)].astype(LOW)
            copy = send(outgoing[level], incoming[level], chain, level, partners[level])
            yield
            copy.wait()
            total[pl.ds(keep, half)] = held[pl.ds(keep, half)] + incoming[level][...].astype(WIDE)
            held, base, size = total, keep, half
            bases.append(keep)
        part = size // count_y
        outgoing[depth][...] = held[pl.ds(base, size)].astype(LOW)
        spread = []
        for k in range(1, count_y):
            peer = lax.rem(me_y + k, count_y)
            source = outgoing[depth].at[pl.ds(peer * part, part)]
            spread.append(send(source, incoming[depth].at[k], chain, 2 * depth + k, (peer, me_z)))
        yield
        own = pl.ds(base + me_y * part, part)
        summed = held[own]
        for k, copy in enumerate(spread):
            copy.wait()
            summed = summed + incoming[depth][k + 1].astype(WIDE)
        sums[own] = summed.astype(LOW)
        spread = []
        for k in range(1, count_y):
            peer = lax.rem(me_y + k, count_y)
            spread.append(
                send(sums.at[own], sums.at[own], chain, 2 * depth + count_y + k, (peer, me_z))
            )
        yield
        for copy in spread:
            copy.wait()
        for level in range(depth - 1, -1, -1):
            span = pl.ds(bases[level], size)
            copy = send(sums.at[span], sums.at[span], chain, depth + level, partners[level])
            yield
            copy.wait()
            size *= 2

    running = []

    def launch(ready):
        for index, entry in enumerate(plan.chains):
            if entry.ready == ready:
                running.append(run_chain(index))
                next(running[-1])

    def advance():
        for work in list(running):
            if next(work, "done") == "done":
                running.remove(work)

    mask = jnp.tile(spread_mask(r.mask_in[...], length), (HEADS, 1))
    for copy in token_copies:
        copy.wait()
    to_lines(r.token_got, r.token_wide)
    for copy in loads[:3]:
        copy.wait()
    token_wide = r.token_wide[...]
    normal, inverse = norm_rows(token_wide)
    r.normal[...] = normal
    r.inverse[...] = inverse
    normed = normal.astype(LOW)
    for piece, target in enumerate((r.query, r.key, r.value)):
        target[...] = dot(normed, r.qkv_weight[:, piece * width : (piece + 1) * width]).astype(LOW)
    for line in range(lines):
        rows = pl.ds(line * length, length)
        query_vec, key_vec = r.query[rows].astype(WIDE), r.key[rows].astype(WIDE)
        query_stack = stack_heads(query_vec * unit_scale(query_vec)).astype(LOW)
        key_unit = (key_vec * unit_scale(key_vec)).astype(LOW)
        weights = mask * jnp.exp(factor * dot(query_stack, key_unit, 1, 1))
        probs = weights / jnp.sum(weights, axis=-1, keepdims=True)
        r.probs[line] = probs
        r.attended[rows] = unstack_heads(dot(probs.astype(LOW), r.value[rows])).astype(LOW)
    field = (r.token_wide[...] + dot(r.attended[...], r.out_weight[...])).astype(LOW)
    r.padded_value[1 : planes + 1, 1 : part_z + 1] = field.reshape(planes, part_z, length, width)
    finish_value = halo(r.padded_value, 0)

    for copy in grad_copies:
        copy.wait()
    to_lines(r.grad_got, r.above_wide)
    for copy in loads[3:]:
        copy.wait()
    r.grad_pre[...] = dot(r.above_wide[...].astype(LOW), r.down_weight[...]).astype(LOW)
    finish_value()
    for line in range(lines):
        plane, column = line // part_z, line % part_z
        rows = pl.ds(line * length, length)
        centre = r.padded_value[plane + 1, column + 1].astype(WIDE)
        r.mixed[rows] = (centre + conv_line(r.padded_value, r.taps, plane, column, False)).astype(LOW)
    group = min(2, part_z)
    for start in range(0, lines, group):
        plane, columns = start // part_z, pl.ds(start % part_z + 1, group)
        rows = pl.ds(start * length, group * length)
        mixed_wide = r.mixed[rows].astype(WIDE)
        normal, inverse = norm_rows(mixed_wide)
        r.normed[rows] = normal.astype(LOW)
        pre_act = dot(r.normed[rows], r.up_weight[...])
        square = pre_act * pre_act
        tangent = jnp.tanh(GELU_SLOPE * (pre_act + GELU_CUBIC * square * pre_act))
        r.hidden[rows] = (0.5 * pre_act * (1.0 + tangent)).astype(LOW)
        slope = 0.5 * (1.0 + tangent) + 0.5 * pre_act * (1.0 - tangent * tangent) * GELU_SLOPE * (
            1.0 + 3.0 * GELU_CUBIC * square
        )
        r.grad_pre[rows] = (r.grad_pre[rows].astype(WIDE) * slope).astype(LOW)
        r.block_wide[rows] = mixed_wide + dot(r.hidden[rows], r.down_weight[...], 1, 1)
        grad_normed = dot(r.grad_pre[rows], r.up_weight[...], 1, 1)
        r.padded_grad[plane + 1, columns] = (
            (r.above_wide[rows] + norm_rows_back(grad_normed, normal, inverse))
            .astype(LOW)
            .reshape(group, length, width)
        )
    finish_grad = halo(r.padded_grad, 1)
    from_lines(r.block_wide, r.block_sent)
    block_copies = swap(r.block_sent, r.block_out, 2, False)
    r.block_out[me_x] = r.block_sent[me_y]
    put_tiles(r.early, 0, dot(r.normed[...], r.grad_pre[...], 0, 0))
    put_tiles(r.early, plan.tiles, dot(r.above_wide[...].astype(LOW), r.hidden[...], 0, 0))
    launch(0)

    r.tap_sums[...] = jnp.zeros_like(r.tap_sums)
    for line in range(lines):
        plane, column = line // part_z, line % part_z
        centre = r.padded_grad[plane + 1, column + 1].astype(WIDE)
        shifted = (shift_rows(centre, -1), centre, shift_rows(centre, 1))
        for a in range(3):
            for d in range(3):
                window = r.padded_value[plane + a, column + d].astype(WIDE)
                for b in range(3):
                    product = (shifted[b] * window).reshape(length // 8, 8, width)
                    r.tap_sums[(a * 3 + b) * 3 + d] += jnp.sum(product, axis=0)
    r.tap_flat[...] = jnp.zeros_like(r.tap_flat)
    r.tap_flat[:27, :width] = jnp.sum(r.tap_sums[...], axis=1)
    put_tiles(r.early, 2 * plan.tiles, r.tap_flat[...])
    finish_grad()
    advance()

    for line in range(lines):
        plane, column = line // part_z, line % part_z
        rows = pl.ds(line * length, length)
        centre = r.padded_grad[plane + 1, column + 1].astype(WIDE)
        r.grad_value[rows] = (
            centre + conv_line(r.padded_grad, r.taps, plane, column, True)
        ).astype(LOW)
    r.above[...] = dot(r.grad_value[...], r.out_weight[...], 1, 1).astype(LOW)
    out_part = dot(r.attended[...], r.grad_value[...], 0, 0)
    put_tiles(r.early, 2 * plan.tiles + plan.tap_tiles, out_part[:, width - 128 :])
    r.joint[:, 3 * width :] = out_part[:, : width - 128]
    if plan.early_pad:
        r.early[plan.early_used :] = jnp.zeros((plan.early_pad, 16, 128), WIDE)
    launch(1)
    advance()
    for line in range(lines):
        rows = pl.ds(line * length, length)
        query_vec, key_vec = r.query[rows].astype(WIDE), r.key[rows].astype(WIDE)
        query_scale, key_scale = unit_scale(query_vec), unit_scale(key_vec)
        query_stack = stack_heads(query_vec * query_scale).astype(LOW)
        key_unit = (key_vec * key_scale).astype(LOW)
        probs = r.probs[line]
        grad_stack = stack_heads(r.above[rows].astype(WIDE)).astype(LOW)
        grad_probs = dot(grad_stack, r.value[rows], 1, 1)
        grad_scores = probs * (grad_probs - jnp.sum(grad_probs * probs, axis=-1, keepdims=True))
        grad_low = (factor * grad_scores).astype(LOW)
        r.grad_v[rows] = dot(probs.astype(LOW), grad_stack, 0, 0).astype(LOW)
        grad_qunit = unstack_heads(dot(grad_low, key_unit))
        grad_kunit = dot(grad_low, query_stack, 0, 0)
        r.grad_q[rows] = unit_back(grad_qunit, query_vec, query_scale).astype(LOW)
        r.grad_k[rows] = unit_back(grad_kunit, key_vec, key_scale).astype(LOW)
        if line == lines // 2:
            advance()
    normal = r.normal[...]
    normed = normal.astype(LOW)
    grad_normed = 0.0
    for piece, grad in enumerate((r.grad_q, r.grad_k, r.grad_v)):
        part = slice(piece * width, (piece + 1) * width)
        grad_normed = grad_normed + dot(grad[...], r.qkv_weight[:, part], 1, 1)
        r.joint[:, part] = dot(normed, grad[...], 0, 0)
    put_tiles(r.late, 0, r.joint[...])
    if plan.late_pad:
        r.late[plan.late_used :] = jnp.zeros((plan.late_pad, 16, 128), WIDE)
    launch(2)
    upstream = grad_normed.astype(LOW).astype(WIDE)
    r.block_wide[...] = r.grad_value[...].astype(WIDE) + norm_rows_back(
        upstream, normal, r.inverse[...]
    )
    for copy in block_copies:
        copy.wait()
    from_lines(r.block_wide, r.token_sent)
    token_copies = swap(r.token_sent, r.token_out, 3, False)
    r.token_out[me_x] = r.token_sent[me_y]
    while running:
        advance()
    for copy in token_copies:
        copy.wait()


def make_plan(count_y, count_z, extents, hidden_width):
    planes, part_y, part_z, width = extents
    devices = count_y * count_z
    depth = len(bits_of(count_z))
    rows = width // 16
    tiles = rows * (hidden_width // 128)
    tap_tiles = 4
    early_used = 2 * tiles + tap_tiles + rows
    late_used = rows * ((4 * width - 128) // 128)
    early = -(-early_used // devices) * devices
    late = -(-late_used // devices) * devices
    chains, buffers = [], []
    units = early // devices
    cuts = sorted({0, units * 2 // 5, units * 4 // 5, units})
    spans = [(True, a * devices, (b - a) * devices) for a, b in zip(cuts, cuts[1:])]
    spans.append((False, 0, late))
    for index, (is_early, base, size) in enumerate(spans):
        halves = [(size >> (level + 1), 16, 128) for level in range(depth)]
        last = size >> depth
        shapes = halves + [(last, 16, 128)] + halves + [(count_y, last // count_y, 16, 128)]
        names = ["chain%d_%d" % (index, i) for i in range(len(shapes))]
        buffers += list(zip(names, shapes))
        ready = 2 if not is_early else (0 if base + size <= 2 * tiles else 1)
        chains.append(
            types.SimpleNamespace(early=is_early, base=base, size=size, buffers=names, ready=ready)
        )
    return types.SimpleNamespace(
        count_y=count_y, count_z=count_z, planes=planes, part_y=part_y, part_z=part_z, width=width,
        hidden=hidden_width, tiles=tiles, tap_tiles=tap_tiles, early=early, late=late,
        early_used=early_used, late_used=late_used, early_pad=early - early_used,
        late_pad=late - late_used, chains=chains, buffers=buffers, depth=depth,
    )


def run_block(plan, tokens, upstream, weights, mask):
    count_y, width, hidden = plan.count_y, plan.width, plan.hidden
    lines, length = plan.planes * plan.part_z, plan.part_y * plan.count_y
    count = lines * length
    blocks = tokens.shape
    padded = (plan.planes + 2, plan.part_z + 2, length, width)

    def low(*shape):
        return pltpu.VMEM(shape, LOW)

    def wide(*shape):
        return pltpu.VMEM(shape, WIDE)

    slots = (len(plan.chains), 2 * plan.depth + 2 * count_y)
    scratch = {
        "load_sem": pltpu.SemaphoreType.DMA((len(weights),)),
        "swap_send": pltpu.SemaphoreType.DMA((4, count_y)),
        "swap_recv": pltpu.SemaphoreType.DMA((4, count_y)),
        "halo_send": pltpu.SemaphoreType.DMA((2, 8)),
        "halo_recv": pltpu.SemaphoreType.DMA((2, 8)),
        "chain_send": pltpu.SemaphoreType.DMA(slots),
        "chain_recv": pltpu.SemaphoreType.DMA(slots),
        "qkv_weight": low(width, 3 * width),
        "out_weight": low(width, width),
        "taps": wide(3, 3, 3, width),
        "up_weight": low(width, hidden),
        "down_weight": low(width, hidden),
        "token_got": low(*blocks),
        "grad_got": low(*blocks),
        "block_sent": low(*blocks),
        "token_sent": low(*blocks),
        "token_wide": wide(count, width),
        "above_wide": wide(count, width),
        "block_wide": wide(count, width),
        "normal": wide(count, width),
        "inverse": wide(count, 1),
        "query": low(count, width),
        "key": low(count, width),
        "value": low(count, width),
        "attended": low(count, width),
        "probs": wide(lines, HEADS * length, length),
        "padded_value": low(*padded),
        "padded_grad": low(*padded),
        "mixed": low(count, width),
        "normed": low(count, width),
        "hidden": low(count, hidden),
        "grad_pre": low(count, hidden),
        "tap_sums": wide(27, 8, width),
        "tap_flat": wide(32, 256),
        "grad_value": low(count, width),
        "above": low(count, width),
        "grad_q": low(count, width),
        "grad_k": low(count, width),
        "grad_v": low(count, width),
        "joint": wide(width, 4 * width - 128),
        "early": wide(plan.early, 16, 128),
        "early_total": wide(plan.early, 16, 128),
        "late": wide(plan.late, 16, 128),
        "late_total": wide(plan.late, 16, 128),
    }
    for name, shape in plan.buffers:
        scratch[name] = low(*shape)
    names = ["token_in", "grad_in", "qkv_in", "out_in", "taps_in", "up_in", "down_in", "mask_in"]
    outs = {
        "block_out": jax.ShapeDtypeStruct(blocks, LOW),
        "token_out": jax.ShapeDtypeStruct(blocks, LOW),
        "early_sums": jax.ShapeDtypeStruct((plan.early, 16, 128), LOW),
        "late_sums": jax.ShapeDtypeStruct((plan.late, 16, 128), LOW),
    }
    plan.names = names + list(outs) + list(scratch)
    return pl.pallas_call(
        functools.partial(block_kernel, plan),
        out_shape=tuple(outs.values()),
        in_specs=[VMEM, VMEM] + [ANY] * len(weights) + [VMEM],
        out_specs=(VMEM,) * len(outs),
        scratch_shapes=list(scratch.values()),
        compiler_params=pltpu.CompilerParams(
            collective_id=0, has_side_effects=True, vmem_limit_bytes=48 * 1024 * 1024
        ),
        name="block",
    )(tokens, upstream, *weights, mask)


def finish_kernel(plan, factor, early, late, qkv_out, out_out, kernel_out, up_out, down_out, joint):
    rows = plan.width // 16

    def tile(source, index):
        return source[index * rows : (index + 1) * rows].astype(WIDE).reshape(plan.width, 128) * factor

    for index in range(plan.hidden // 128):
        columns = slice(index * 128, (index + 1) * 128)
        up_out[:, columns] = tile(early, index)
        down_out[:, columns] = tile(early, plan.hidden // 128 + index)
    for index in range(plan.late_used // rows):
        joint[:, index * 128 : (index + 1) * 128] = tile(late, index)
    qkv_out[...] = joint[:, : 3 * plan.width]
    tail = early[2 * plan.tiles + plan.tap_tiles : plan.early_used].astype(WIDE) * factor
    out_out[...] = jnp.concatenate(
        [joint[:, 3 * plan.width :], tail.reshape(plan.width, 128)], axis=1
    )
    taps = early[2 * plan.tiles : 2 * plan.tiles + plan.tap_tiles].astype(WIDE) * factor
    flat = jnp.concatenate([taps[:2].reshape(32, 128), taps[2:].reshape(32, 128)], axis=1)
    for a in range(3):
        for b in range(3):
            first = (a * 3 + b) * 3
            kernel_out[a, b] = flat[first : first + 3, : plan.width]


def finish(plan, factor, early, late):
    width, hidden = plan.width, plan.hidden
    shapes = ((width, 3 * width), (width, width), (3, 3, 3, width), (width, hidden), (width, hidden))
    return pl.pallas_call(
        functools.partial(finish_kernel, plan, factor),
        out_shape=tuple(jax.ShapeDtypeStruct(shape, WIDE) for shape in shapes),
        in_specs=[VMEM, VMEM],
        out_specs=(VMEM,) * len(shapes),
        scratch_shapes=[pltpu.VMEM((width, 4 * width - 128), WIDE)],
        compiler_params=pltpu.CompilerParams(vmem_limit_bytes=16 * 1024 * 1024),
        name="finish",
    )(early, late)


def local(tokens, qkv_weight, out_weight, conv_kernel, up_weight, down_weight, band_mask, grad_out):
    count_y, count_z = lax.axis_size("gy"), lax.axis_size("gz")
    extent_x, part_y, part_z, width = tokens.shape
    planes = extent_x // count_y
    plan = make_plan(count_y, count_z, (planes, part_y, part_z, width), up_weight.shape[1])
    blocks = (count_y, planes * part_y, part_z * width)
    weights = (qkv_weight, out_weight, conv_kernel, up_weight, down_weight.T)
    block_out, token_gradient, early, late = run_block(
        plan, tokens.reshape(blocks), grad_out.reshape(blocks), weights, band_mask
    )
    factor = 1.0 / math.sqrt(extent_x * part_y * count_y * part_z * count_z)
    qkv_sum, out_sum, kernel_sum, up_sum, down_sum = finish(plan, factor, early, late)
    return (
        block_out.reshape(tokens.shape),
        token_gradient.reshape(tokens.shape),
        qkv_sum,
        out_sum,
        kernel_sum,
        up_sum,
        down_sum.T,
    )


def solution(mesh):
    placed = (P(None, "gy", "gz", None), P(), P(), P(), P(), P(), P(), P(None, "gy", "gz", None))
    return jax.shard_map(
        local,
        mesh=mesh,
        in_specs=placed,
        out_specs=(P(None, "gy", "gz", None), P(None, "gy", "gz", None), P(), P(), P(), P(), P()),
        check_vma=False,
    )
```

```python
import functools
import math
import types

import jax
import jax.numpy as jnp
from jax import lax
from jax.experimental import pallas as pl
from jax.experimental.pallas import tpu as pltpu
from jax.sharding import PartitionSpec as P

HEADS = 6
BLOCK = 16


NORM_EPS = 1e-05
UNIT_EPS = 1e-06
GELU_SLOPE = 0.7978845608028654
GELU_CUBIC = 0.044715

MESH = pl.DeviceIdType.MESH
VMEM = pl.BlockSpec(memory_space=pltpu.VMEM)
SMEM = pl.BlockSpec(memory_space=pltpu.SMEM)
LOW = jnp.bfloat16
WIDE = jnp.float32


def norm_rows(values):
    centred = values - jnp.mean(values, axis=-1, keepdims=True)
    inverse = lax.rsqrt(jnp.mean(centred * centred, axis=-1, keepdims=True) + NORM_EPS)
    return (centred * inverse, inverse)


def norm_rows_back(upstream, normal, inverse):
    return inverse * (
        upstream
        - jnp.mean(upstream, axis=-1, keepdims=True)
        - normal * jnp.mean(upstream * normal, axis=-1, keepdims=True)
    )


def unit_scale(values):
    return lax.rsqrt(jnp.mean(values * values, axis=-1, keepdims=True) + UNIT_EPS)


def unit_back(upstream, values, scaling):
    return scaling * upstream - scaling * scaling * scaling * values * jnp.mean(
        upstream * values, axis=-1, keepdims=True
    )


def place_of(index):
    return index + (1 - 2 * lax.rem(index, 2)) * lax.rem(index // 2, 2)


def dot(left, right, left_axis=1, right_axis=0):
    return lax.dot_general(
        left, right, (((left_axis,), (right_axis,)), ((), ())), preferred_element_type=WIDE
    )


def stack_heads(values):
    width = values.shape[1]
    head_of = lax.broadcasted_iota(jnp.int32, (1, width), 1) // (width // HEADS)
    return jnp.concatenate([jnp.where(head_of == h, values, 0.0) for h in range(HEADS)], axis=0)


def unstack_heads(stacked):
    rows, width = stacked.shape[0] // HEADS, stacked.shape[1]
    head_of = lax.broadcasted_iota(jnp.int32, (1, width), 1) // (width // HEADS)
    joined = stacked[:rows]
    for h in range(1, HEADS):
        joined = jnp.where(head_of == h, stacked[h * rows : (h + 1) * rows], joined)
    return joined


def shift_rows(values, step):
    return pltpu.roll(values, step % values.shape[0], 0)


def face(step, extent):
    return {
        0: (pl.ds(0, extent), pl.ds(1, extent)),
        1: (pl.ds(extent - 1, 1), pl.ds(0, 1)),
        -1: (pl.ds(0, 1), pl.ds(extent + 1, 1)),
    }[step]


def conv_line(padded, taps, plane, column, flip, inside):
    by_shift = [None, None, None]
    for a in range(3):
        for d in range(3):
            x, z = plane + a, column + d
            here = 0 < x < padded.shape[0] - 1 and 0 < z < padded.shape[1] - 1
            if here != inside:
                continue
            window = padded[x, z].astype(WIDE)
            for b in range(3):
                tap = taps[2 - a, 2 - b, 2 - d : 3 - d] if flip else taps[a, b, d : d + 1]
                term = tap * window
                by_shift[b] = term if by_shift[b] is None else by_shift[b] + term
    if by_shift[0] is None:
        return 0.0
    return shift_rows(by_shift[0], 1) + by_shift[1] + shift_rows(by_shift[2], -1)


def put_tiles(target, base, matrix):
    rows = matrix.shape[0] // 16
    for column in range(matrix.shape[1] // 128):
        target[base + column * rows : base + (column + 1) * rows] = matrix[
            :, column * 128 : (column + 1) * 128
        ].reshape(rows, 16, 128)


def spread_mask(mask, length):
    blocks = length // BLOCK
    column = lax.broadcasted_iota(jnp.int32, (BLOCK, length), 1) // BLOCK
    rows = []
    for i in range(blocks):
        row = jnp.zeros((BLOCK, length), jnp.int32)
        for j in range(blocks):
            row = jnp.where(column == j, mask[i, j], row)
        rows.append(row)
    return jnp.concatenate(rows, axis=0).astype(WIDE)


def block_kernel(plan, *refs):
    r = types.SimpleNamespace(**dict(zip(plan.names, refs)))
    count_y, count_z = plan.count_y, plan.count_z
    planes, part_y, part_z, width = plan.planes, plan.part_y, plan.part_z, plan.width
    lines, length = planes * part_z, part_y * count_y
    count = lines * length
    factor = 2.0 / math.sqrt(width // HEADS)
    me_y, me_z = lax.axis_index("gy"), lax.axis_index("gz")
    me_x = place_of(me_y)

    steps = [(-1, 0), (1, 0), (0, -1), (0, 1), (-1, -1), (-1, 1), (1, -1), (1, 1)]
    half_z = max(1, count_z // 2)
    flip = me_y + 1 - 2 * lax.rem(me_y, 2)
    friends = [(lax.rem(me_y + k, count_y), me_z) for k in range(1, count_y)]
    friends += [(me_y, me_z + 1 - 2 * lax.rem(me_z, 2))]
    friends += [
        (peer, lax.rem(me_z + 2 * k, count_z)) for k in range(1, half_z) for peer in (me_y, flip)
    ]
    barrier = pltpu.get_barrier_semaphore()

    def reach(dx, action):
        if dx == 0:
            action()
        elif dx == 1:
            pl.when(me_x < count_y - 1)(action)
        else:
            pl.when(me_x > 0)(action)

    def place(dx, dz):
        return (place_of(me_x + dx), lax.rem(me_z + dz + count_z, count_z))

    def greet(peer):
        pl.semaphore_signal(barrier, inc=1, device_id=peer, device_id_type=MESH)

    for peer in friends:
        greet(peer)
    for dx, dz in steps:
        if dz != 0:
            reach(dx, lambda dx=dx, dz=dz: greet(place(dx, dz)))
    common = len(friends)
    inner = (me_x > 0) & (me_x < count_y - 1)

    @pl.when(inner)
    def _():
        pl.semaphore_wait(barrier, common + 6)

    @pl.when(jnp.logical_not(inner))
    def _():
        pl.semaphore_wait(barrier, common + 4)

    def swap(source, target, slot, inward, first=1, last=count_y):
        copies = []
        for k in range(first, last):
            peer = lax.rem(me_y + k, count_y)
            copy = pltpu.make_async_remote_copy(
                src_ref=source.at[place_of(peer) if inward else peer],
                dst_ref=target.at[me_y if inward else me_x],
                send_sem=r.swap_send.at[slot, k],
                recv_sem=r.swap_recv.at[slot, k],
                device_id=(peer, me_z),
                device_id_type=MESH,
            )
            copy.start()
            copies.append(copy)
        return copies

    token_copies = swap(r.token_in, r.token_got, 0, True)
    grad_copies = swap(r.grad_in, r.grad_got, 1, True, 1, count_y // 2)
    r.token_got[me_y] = r.token_in[me_x]
    r.grad_got[me_y] = r.grad_in[me_x]

    def to_lines(got, target):
        for p in range(count_y):
            block = got[p].astype(WIDE)
            for line in range(lines):
                x, z = line // part_z, line % part_z
                target[pl.ds(line * length + p * part_y, part_y)] = block[
                    x * part_y : (x + 1) * part_y, z * width : (z + 1) * width
                ]

    def from_lines(source, target):
        for p in range(count_y):
            rows = [
                jnp.concatenate(
                    [
                        source[pl.ds((x * part_z + z) * length + p * part_y, part_y)]
                        for z in range(part_z)
                    ],
                    axis=1,
                )
                for x in range(planes)
            ]
            target[p] = (rows[0] if planes == 1 else jnp.concatenate(rows, axis=0)).astype(LOW)

    def conv_inside(padded, flip):
        for line in range(lines):
            plane, column = line // part_z, line % part_z
            r.conv_part[pl.ds(line * length, length)] = padded[plane + 1, column + 1].astype(
                WIDE
            ) + conv_line(padded, r.taps, plane, column, flip, True)

    def conv_rest(padded, line, flip):
        return r.conv_part[pl.ds(line * length, length)] + conv_line(
            padded, r.taps, line // part_z, line % part_z, flip, False
        )

    def halo(padded, slot):
        copies = []
        for index, (dx, dz) in enumerate(steps):
            from_x, to_x = face(dx, planes)
            from_z, to_z = face(dz, part_z)
            inside_x = pl.ds(from_x.start + 1, from_x.size)
            inside_z = pl.ds(from_z.start + 1, from_z.size)
            copies.append(
                lambda index=index, dx=dx, dz=dz, ix=inside_x, iz=inside_z, tx=to_x, tz=to_z: pltpu.make_async_remote_copy(
                    src_ref=padded.at[ix, iz],
                    dst_ref=padded.at[tx, tz],
                    send_sem=r.halo_send.at[slot, index],
                    recv_sem=r.halo_recv.at[slot, index],
                    device_id=place(dx, dz),
                    device_id_type=MESH,
                )
            )
        for index, (dx, dz) in enumerate(steps):
            reach(dx, lambda index=index: copies[index]().start())
        blank = jnp.zeros((1,) + tuple(padded.shape[1:]), padded.dtype)

        @pl.when(me_x == 0)
        def _():
            padded[0:1] = blank

        @pl.when(me_x == count_y - 1)
        def _():
            padded[planes + 1 : planes + 2] = blank

        def finish():
            for index, (dx, dz) in enumerate(steps):
                reach(dx, lambda index=index: copies[index]().wait_send())
                reach(-dx, lambda index=index: copies[index]().wait_recv())

        return finish

    me_core, me_chip = lax.rem(me_z, 2), me_z // 2

    me_even, me_far = lax.rem(me_y, 2), me_y // 2
    far = count_y // 2

    def sibling(k):
        peer = lax.rem(me_core + k, 2)
        return peer, (me_y, me_chip * 2 + peer)

    def near(k):
        even = lax.rem(me_even + k // half_z, 2)
        chip = lax.rem(me_chip + k % half_z, half_z)
        return even * half_z + chip, (me_far * 2 + even, chip * 2 + me_core)

    def distant(k):
        peer = lax.rem(me_far + k, far)
        return peer, (peer * 2 + me_even, me_z)

    groups = (
        (2, me_core, sibling),
        (2 * half_z, me_even * half_z + me_chip, near),
        (far, me_far, distant),
    )

    def send(source, target, chain, stage, k, peer):
        copy = pltpu.make_async_remote_copy(
            src_ref=source,
            dst_ref=target,
            send_sem=r.chain_send.at[chain, stage, k],
            recv_sem=r.chain_recv.at[chain, stage, k],
            device_id=peer,
            device_id_type=MESH,
        )
        copy.start()
        return copy

    def run_chain(chain):
        entry = plan.chains[chain]
        sums = r.sums
        base, size = entry.base, entry.size
        held, first = r.parts, base
        spans = []
        for level, (total, me, peer_of) in enumerate(groups):
            outgoing, incoming, result = (getattr(r, name) for name in entry.buffers[level])
            part = size // total
            outgoing[...] = held[pl.ds(first, size)].astype(LOW)
            copies = []
            for k in range(1, total):
                index, peer = peer_of(k)
                copies.append(
                    send(
                        outgoing.at[pl.ds(index * part, part)], incoming.at[k], chain, level, k, peer
                    )
                )
            yield
            summed = held[pl.ds(first + me * part, part)]
            for k, copy in enumerate(copies):
                copy.wait()
                summed = summed + incoming[k + 1].astype(WIDE)
            result[...] = summed
            held, first = result, 0
            base, size = base + me * part, part
            spans.append((base, size))
        sums[pl.ds(base, size)] = held[...].astype(LOW)
        for level in range(len(groups) - 1, -1, -1):
            total, _, peer_of = groups[level]
            span = pl.ds(*spans[level])
            copies = [
                send(sums.at[span], sums.at[span], chain, len(groups) + level, k, peer_of(k)[1])
                for k in range(1, total)
            ]
            yield
            for copy in copies:
                copy.wait()

    running = []

    def launch(chain):
        if plan.chains[chain]:
            running.append(run_chain(chain))
            next(running[-1])

    def advance():
        for work in list(reversed(running)):
            if next(work, "done") == "done":
                running.remove(work)

    mask = jnp.tile(spread_mask(r.mask, length), (HEADS, 1))
    for copy in token_copies:
        copy.wait()
    to_lines(r.token_got, r.token_wide)
    token_wide = r.token_wide[...]
    normal, inverse = norm_rows(token_wide)
    r.normal[...] = normal
    r.inverse[...] = inverse
    normed = normal.astype(LOW)
    for piece, target in enumerate((r.query, r.key, r.value)):
        target[...] = dot(normed, r.qkv_weight[:, piece * width : (piece + 1) * width]).astype(LOW)
    for line in range(lines):
        rows = pl.ds(line * length, length)
        query_vec, key_vec = r.query[rows].astype(WIDE), r.key[rows].astype(WIDE)
        query_stack = stack_heads(query_vec * unit_scale(query_vec)).astype(LOW)
        key_unit = (key_vec * unit_scale(key_vec)).astype(LOW)
        weights = mask * jnp.exp(factor * dot(query_stack, key_unit, 1, 1))
        probs = weights / jnp.sum(weights, axis=-1, keepdims=True)
        r.probs[line] = probs
        r.attended[rows] = unstack_heads(dot(probs.astype(LOW), r.value[rows])).astype(LOW)
    field = (r.token_wide[...] + dot(r.attended[...], r.out_weight[...])).astype(LOW)
    r.padded_value[1 : planes + 1, 1 : part_z + 1] = field.reshape(planes, part_z, length, width)
    finish_value = halo(r.padded_value, 0)
    grad_copies += swap(r.grad_in, r.grad_got, 1, True, count_y // 2)

    conv_inside(r.padded_value, False)
    finish_value()
    for line in range(lines):
        r.mixed[pl.ds(line * length, length)] = conv_rest(r.padded_value, line, False).astype(LOW)
    group = min(2, part_z)
    for start in range(0, lines, group):
        rows = pl.ds(start * length, group * length)
        mixed_wide = r.mixed[rows].astype(WIDE)
        normal, inverse = norm_rows(mixed_wide)
        r.normal_second[rows] = normal
        r.inverse_second[rows] = inverse
        r.normed[rows] = normal.astype(LOW)
        pre_act = dot(r.normed[rows], r.up_weight[...])
        square = pre_act * pre_act
        tangent = jnp.tanh(GELU_SLOPE * (pre_act + GELU_CUBIC * square * pre_act))
        r.hidden[rows] = (0.5 * pre_act * (1.0 + tangent)).astype(LOW)
        r.slope[rows] = 0.5 * (1.0 + tangent) + 0.5 * pre_act * (
            1.0 - tangent * tangent
        ) * GELU_SLOPE * (1.0 + 3.0 * GELU_CUBIC * square)
        r.block_wide[rows] = mixed_wide + dot(r.hidden[rows], r.down_weight[...], 1, 1)

    for copy in grad_copies:
        copy.wait()
    to_lines(r.grad_got, r.above_wide)
    for start in range(0, lines, group):
        plane, columns = start // part_z, pl.ds(start % part_z + 1, group)
        rows = pl.ds(start * length, group * length)
        grad_hidden = dot(r.above_wide[rows].astype(LOW), r.down_weight[...]).astype(LOW)
        r.grad_pre[rows] = (grad_hidden.astype(WIDE) * r.slope[rows]).astype(LOW)
        grad_normed = dot(r.grad_pre[rows], r.up_weight[...], 1, 1)
        r.padded_grad[plane + 1, columns] = (
            (
                r.above_wide[rows]
                + norm_rows_back(grad_normed, r.normal_second[rows], r.inverse_second[rows])
            )
            .astype(LOW)
            .reshape(group, length, width)
        )
    finish_grad = halo(r.padded_grad, 1)
    put_tiles(r.parts, 0, dot(r.normed[...], r.grad_pre[...], 0, 0))
    put_tiles(r.parts, plan.tiles, dot(r.above_wide[...].astype(LOW), r.hidden[...], 0, 0))
    launch(0)

    r.tap_sums[...] = jnp.zeros_like(r.tap_sums)
    for line in range(lines):
        plane, column = line // part_z, line % part_z
        centre = r.padded_grad[plane + 1, column + 1].astype(WIDE)
        shifted = (shift_rows(centre, -1), centre, shift_rows(centre, 1))
        for a in range(3):
            for d in range(3):
                window = r.padded_value[plane + a, column + d].astype(WIDE)
                for b in range(3):
                    product = (shifted[b] * window).reshape(length // 8, 8, width)
                    r.tap_sums[(a * 3 + b) * 3 + d] += jnp.sum(product, axis=0)
    r.tap_flat[...] = jnp.zeros_like(r.tap_flat)
    r.tap_flat[:27, :width] = jnp.sum(r.tap_sums[...], axis=1)
    put_tiles(r.parts, 2 * plan.tiles, r.tap_flat[...])
    if plan.pad:
        r.parts[plan.used :] = jnp.zeros((plan.pad, 16, 128), WIDE)
    from_lines(r.block_wide, r.block_sent)
    conv_inside(r.padded_grad, True)
    advance()
    finish_grad()
    block_copies = swap(r.block_sent, r.block_out, 2, False)
    r.block_out[me_x] = r.block_sent[me_y]

    for line in range(lines):
        r.grad_value[pl.ds(line * length, length)] = conv_rest(r.padded_grad, line, True).astype(LOW)
    r.above[...] = dot(r.grad_value[...], r.out_weight[...], 1, 1).astype(LOW)
    r.joint[:, 3 * width :] = dot(r.attended[...], r.grad_value[...], 0, 0)
    for line in range(lines):
        rows = pl.ds(line * length, length)
        query_vec, key_vec = r.query[rows].astype(WIDE), r.key[rows].astype(WIDE)
        query_scale, key_scale = unit_scale(query_vec), unit_scale(key_vec)
        query_stack = stack_heads(query_vec * query_scale).astype(LOW)
        key_unit = (key_vec * key_scale).astype(LOW)
        probs = r.probs[line]
        grad_stack = stack_heads(r.above[rows].astype(WIDE)).astype(LOW)
        grad_probs = dot(grad_stack, r.value[rows], 1, 1)
        grad_scores = probs * (grad_probs - jnp.sum(grad_probs * probs, axis=-1, keepdims=True))
        grad_low = (factor * grad_scores).astype(LOW)
        r.grad_v[rows] = dot(probs.astype(LOW), grad_stack, 0, 0).astype(LOW)
        grad_qunit = unstack_heads(dot(grad_low, key_unit))
        grad_kunit = dot(grad_low, query_stack, 0, 0)
        r.grad_q[rows] = unit_back(grad_qunit, query_vec, query_scale).astype(LOW)
        r.grad_k[rows] = unit_back(grad_kunit, key_vec, key_scale).astype(LOW)
    advance()
    normal = r.normal[...]
    normed = normal.astype(LOW)
    pieces = [
        (slice(piece * width, (piece + 1) * width), grad)
        for piece, grad in enumerate((r.grad_q, r.grad_k, r.grad_v))
    ]
    for part, grad in pieces:
        r.joint[:, part] = dot(normed, grad[...], 0, 0)
    put_tiles(r.parts, 2 * plan.tiles + plan.tap_tiles, r.joint[...])
    launch(1)
    grad_normed = 0.0
    for part, grad in pieces:
        grad_normed = grad_normed + dot(grad[...], r.qkv_weight[:, part], 1, 1)
    upstream = grad_normed.astype(LOW).astype(WIDE)
    r.block_wide[...] = r.grad_value[...].astype(WIDE) + norm_rows_back(
        upstream, normal, r.inverse[...]
    )
    for copy in block_copies:
        copy.wait()
    from_lines(r.block_wide, r.token_sent)
    token_copies = swap(r.token_sent, r.token_out, 3, False)
    r.token_out[me_x] = r.token_sent[me_y]
    while running:
        advance()
    for copy in token_copies:
        copy.wait()


def make_plan(count_y, count_z, extents, hidden_width):
    planes, part_y, part_z, width = extents
    devices = count_y * count_z
    rows = width // 16
    tiles = rows * (hidden_width // 128)
    tap_tiles = 4
    used = 2 * tiles + tap_tiles + rows * (4 * width // 128)
    whole = -(-used // devices) * devices
    chains, buffers = [], []
    cut = 2 * tiles // devices * devices
    sizes = (2, count_z // 2 * 2, count_y // 2)
    for index, (base, size) in enumerate(((0, cut), (cut, whole - cut))):
        names, left = [], size
        for level, total in enumerate(sizes):
            part = left // total
            names.append(["chain%d_%s%d" % (index, kind, level) for kind in ("out", "in", "sum")])
            shapes = ((left, 16, 128), (total, part, 16, 128), (part, 16, 128))
            buffers += list(zip(names[-1], shapes, (LOW, LOW, WIDE))) if size else []
            left = part
        chains.append(types.SimpleNamespace(base=base, size=size, buffers=names) if size else None)
    return types.SimpleNamespace(
        count_y=count_y, count_z=count_z, planes=planes, part_y=part_y, part_z=part_z, width=width,
        hidden=hidden_width, tiles=tiles, tap_tiles=tap_tiles, used=used, whole=whole,
        pad=whole - used, chains=chains, buffers=buffers, most=max(sizes), levels=len(sizes),
    )


def run_block(plan, tokens, upstream, weights, mask):
    count_y, width, hidden = plan.count_y, plan.width, plan.hidden
    lines, length = plan.planes * plan.part_z, plan.part_y * plan.count_y
    count = lines * length
    blocks = tokens.shape
    padded = (plan.planes + 2, plan.part_z + 2, length, width)

    def low(*shape):
        return pltpu.VMEM(shape, LOW)

    def wide(*shape):
        return pltpu.VMEM(shape, WIDE)

    slots = (len(plan.chains), 2 * plan.levels, plan.most)
    scratch = {
        "swap_send": pltpu.SemaphoreType.DMA((4, count_y)),
        "swap_recv": pltpu.SemaphoreType.DMA((4, count_y)),
        "halo_send": pltpu.SemaphoreType.DMA((2, 8)),
        "halo_recv": pltpu.SemaphoreType.DMA((2, 8)),
        "chain_send": pltpu.SemaphoreType.DMA(slots),
        "chain_recv": pltpu.SemaphoreType.DMA(slots),
        "token_got": low(*blocks),
        "grad_got": low(*blocks),
        "block_sent": low(*blocks),
        "token_sent": low(*blocks),
        "token_wide": wide(count, width),
        "above_wide": wide(count, width),
        "block_wide": wide(count, width),
        "normal": wide(count, width),
        "inverse": wide(count, 1),
        "normal_second": wide(count, width),
        "inverse_second": wide(count, 1),
        "slope": wide(count, hidden),
        "conv_part": wide(count, width),
        "query": low(count, width),
        "key": low(count, width),
        "value": low(count, width),
        "attended": low(count, width),
        "probs": wide(lines, HEADS * length, length),
        "padded_value": low(*padded),
        "padded_grad": low(*padded),
        "mixed": low(count, width),
        "normed": low(count, width),
        "hidden": low(count, hidden),
        "grad_pre": low(count, hidden),
        "tap_sums": wide(27, 8, width),
        "tap_flat": wide(32, 256),
        "grad_value": low(count, width),
        "above": low(count, width),
        "grad_q": low(count, width),
        "grad_k": low(count, width),
        "grad_v": low(count, width),
        "joint": wide(width, 4 * width),
        "parts": wide(plan.whole, 16, 128),
    }
    for name, shape, kind in plan.buffers:
        scratch[name] = pltpu.VMEM(shape, kind)
    names = ["token_in", "grad_in", "qkv_weight", "out_weight", "taps", "up_weight", "down_weight"]
    names.append("mask")
    outs = {
        "block_out": jax.ShapeDtypeStruct(blocks, LOW),
        "token_out": jax.ShapeDtypeStruct(blocks, LOW),
        "sums": jax.ShapeDtypeStruct((plan.whole, 16, 128), LOW),
    }
    plan.names = names + list(outs) + list(scratch)
    return pl.pallas_call(
        functools.partial(block_kernel, plan),
        out_shape=tuple(outs.values()),
        in_specs=[VMEM, VMEM] + [VMEM] * len(weights) + [SMEM],
        out_specs=(VMEM,) * len(outs),
        scratch_shapes=list(scratch.values()),
        compiler_params=pltpu.CompilerParams(
            collective_id=0, has_side_effects=True, vmem_limit_bytes=48 * 1024 * 1024
        ),
        name="block",
    )(tokens, upstream, *weights, mask)


def finish_kernel(plan, factor, sums, qkv_out, out_out, kernel_out, up_out, down_out, joint):
    rows = plan.width // 16

    def tile(first):
        return sums[first : first + rows].astype(WIDE).reshape(plan.width, 128) * factor

    taps_at = 2 * plan.tiles
    joint_at = taps_at + plan.tap_tiles
    for index in range(plan.hidden // 128):
        columns = slice(index * 128, (index + 1) * 128)
        up_out[:, columns] = tile(index * rows)
        down_out[:, columns] = tile(plan.tiles + index * rows)
    for index in range(4 * plan.width // 128):
        joint[:, index * 128 : (index + 1) * 128] = tile(joint_at + index * rows)
    qkv_out[...] = joint[:, : 3 * plan.width]
    out_out[...] = joint[:, 3 * plan.width :]
    taps = sums[taps_at:joint_at].astype(WIDE) * factor
    flat = jnp.concatenate([taps[:2].reshape(32, 128), taps[2:].reshape(32, 128)], axis=1)
    for a in range(3):
        for b in range(3):
            first = (a * 3 + b) * 3
            kernel_out[a, b] = flat[first : first + 3, : plan.width]


def finish(plan, factor, sums):
    width, hidden = plan.width, plan.hidden
    shapes = ((width, 3 * width), (width, width), (3, 3, 3, width), (width, hidden), (width, hidden))
    return pl.pallas_call(
        functools.partial(finish_kernel, plan, factor),
        out_shape=tuple(jax.ShapeDtypeStruct(shape, WIDE) for shape in shapes),
        in_specs=[VMEM],
        out_specs=(VMEM,) * len(shapes),
        scratch_shapes=[pltpu.VMEM((width, 4 * width), WIDE)],
        compiler_params=pltpu.CompilerParams(vmem_limit_bytes=16 * 1024 * 1024),
        name="finish",
    )(sums)


def local(tokens, qkv_weight, out_weight, conv_kernel, up_weight, down_weight, band_mask, grad_out):
    count_y, count_z = lax.axis_size("gy"), lax.axis_size("gz")
    extent_x, part_y, part_z, width = tokens.shape
    planes = extent_x // count_y
    plan = make_plan(count_y, count_z, (planes, part_y, part_z, width), up_weight.shape[1])
    blocks = (count_y, planes * part_y, part_z * width)
    weights = (qkv_weight, out_weight, conv_kernel, up_weight, down_weight.T)
    block_out, token_gradient, sums = run_block(
        plan, tokens.reshape(blocks), grad_out.reshape(blocks), weights, band_mask
    )
    factor = 1.0 / math.sqrt(extent_x * part_y * count_y * part_z * count_z)
    qkv_sum, out_sum, kernel_sum, up_sum, down_sum = finish(plan, factor, sums)
    return (
        block_out.reshape(tokens.shape),
        token_gradient.reshape(tokens.shape),
        qkv_sum,
        out_sum,
        kernel_sum,
        up_sum,
        down_sum.T,
    )


def solution(mesh):
    placed = (P(None, "gy", "gz", None), P(), P(), P(), P(), P(), P(), P(None, "gy", "gz", None))
    return jax.shard_map(
        local,
        mesh=mesh,
        in_specs=placed,
        out_specs=(P(None, "gy", "gz", None), P(None, "gy", "gz", None), P(), P(), P(), P(), P()),
        check_vma=False,
    )
```

```python
import functools
import math
import types

import jax
import jax.numpy as jnp
from jax import lax
from jax.experimental import pallas as pl
from jax.experimental.pallas import tpu as pltpu
from jax.sharding import PartitionSpec as P

HEADS = 6
BLOCK = 16


NORM_EPS = 1e-05
UNIT_EPS = 1e-06
GELU_SLOPE = 0.7978845608028654
GELU_CUBIC = 0.044715

MESH = pl.DeviceIdType.MESH
SMEM = pl.BlockSpec(memory_space=pltpu.SMEM)
ANY = pl.BlockSpec(memory_space=pl.ANY)
LOW = jnp.bfloat16
WIDE = jnp.float32


def norm_rows(values):
    centred = values - jnp.mean(values, axis=-1, keepdims=True)
    inverse = lax.rsqrt(jnp.mean(centred * centred, axis=-1, keepdims=True) + NORM_EPS)
    return (centred * inverse, inverse)


def norm_rows_back(upstream, normal, inverse):
    return inverse * (
        upstream
        - jnp.mean(upstream, axis=-1, keepdims=True)
        - normal * jnp.mean(upstream * normal, axis=-1, keepdims=True)
    )


def unit_scale(values):
    return lax.rsqrt(jnp.mean(values * values, axis=-1, keepdims=True) + UNIT_EPS)


def unit_back(upstream, values, scaling):
    return scaling * upstream - scaling * scaling * scaling * values * jnp.mean(
        upstream * values, axis=-1, keepdims=True
    )


def place_of(index):
    return index + (1 - 2 * lax.rem(index, 2)) * lax.rem(index // 2, 2)


def dot(left, right, left_axis=1, right_axis=0):
    return lax.dot_general(
        left, right, (((left_axis,), (right_axis,)), ((), ())), preferred_element_type=WIDE
    )


def stack_heads(values):
    width = values.shape[1]
    head_of = lax.broadcasted_iota(jnp.int32, (1, width), 1) // (width // HEADS)
    return jnp.concatenate([jnp.where(head_of == h, values, 0.0) for h in range(HEADS)], axis=0)


def unstack_heads(stacked):
    rows, width = stacked.shape[0] // HEADS, stacked.shape[1]
    head_of = lax.broadcasted_iota(jnp.int32, (1, width), 1) // (width // HEADS)
    joined = stacked[:rows]
    for h in range(1, HEADS):
        joined = jnp.where(head_of == h, stacked[h * rows : (h + 1) * rows], joined)
    return joined


def shift_rows(values, step):
    return pltpu.roll(values, step % values.shape[0], 0)


def face(step, extent):
    return {
        0: (pl.ds(0, extent), pl.ds(1, extent)),
        1: (pl.ds(extent - 1, 1), pl.ds(0, 1)),
        -1: (pl.ds(0, 1), pl.ds(extent + 1, 1)),
    }[step]


def conv_line(padded, taps, plane, column, flip, inside):
    by_shift = [None, None, None]
    for a in range(3):
        for d in range(3):
            x, z = plane + a, column + d
            here = 0 < x < padded.shape[0] - 1 and 0 < z < padded.shape[1] - 1
            if here != inside:
                continue
            window = padded[x, z].astype(WIDE)
            for b in range(3):
                tap = taps[2 - a, 2 - b, 2 - d : 3 - d] if flip else taps[a, b, d : d + 1]
                term = tap * window
                by_shift[b] = term if by_shift[b] is None else by_shift[b] + term
    if by_shift[0] is None:
        return 0.0
    return shift_rows(by_shift[0], 1) + by_shift[1] + shift_rows(by_shift[2], -1)


def put_tiles(target, base, matrix):
    rows = matrix.shape[0] // 16
    for column in range(matrix.shape[1] // 128):
        target[base + column * rows : base + (column + 1) * rows] = matrix[
            :, column * 128 : (column + 1) * 128
        ].reshape(rows, 16, 128)


def spread_mask(mask, length):
    blocks = length // BLOCK
    column = lax.broadcasted_iota(jnp.int32, (BLOCK, length), 1) // BLOCK
    rows = []
    for i in range(blocks):
        row = jnp.zeros((BLOCK, length), jnp.int32)
        for j in range(blocks):
            row = jnp.where(column == j, mask[i, j], row)
        rows.append(row)
    return jnp.concatenate(rows, axis=0).astype(WIDE)


def block_kernel(plan, *refs):
    r = types.SimpleNamespace(**dict(zip(plan.names, refs)))
    count_y, count_z = plan.count_y, plan.count_z
    planes, part_y, part_z, width = plan.planes, plan.part_y, plan.part_z, plan.width
    lines, length = planes * part_z, part_y * count_y
    count = lines * length
    factor = 2.0 / math.sqrt(width // HEADS)
    me_y, me_z = lax.axis_index("gy"), lax.axis_index("gz")
    me_x = place_of(me_y)

    moved = (
        (r.token_slab, r.token_local),
        (r.grad_slab, r.grad_local),
        (r.qkv_hbm, r.qkv_weight),
        (r.out_hbm, r.out_weight),
        (r.taps_hbm, r.taps),
        (r.up_hbm, r.up_weight),
        (r.down_hbm, r.down_weight),
    )
    loads = [
        pltpu.make_async_copy(source, target, r.load_sem.at[index])
        for index, (source, target) in enumerate(moved)
    ]
    for copy in loads:
        copy.start()

    steps = [(-1, 0), (1, 0), (0, -1), (0, 1), (-1, -1), (-1, 1), (1, -1), (1, 1)]
    half_z = max(1, count_z // 2)
    flip = me_y + 1 - 2 * lax.rem(me_y, 2)
    friends = [(lax.rem(me_y + k, count_y), me_z) for k in range(1, count_y)]
    friends += [(me_y, me_z + 1 - 2 * lax.rem(me_z, 2))]
    friends += [
        (peer, lax.rem(me_z + 2 * k, count_z)) for k in range(1, half_z) for peer in (me_y, flip)
    ]
    barrier = pltpu.get_barrier_semaphore()

    def reach(dx, action):
        if dx == 0:
            action()
        elif dx == 1:
            pl.when(me_x < count_y - 1)(action)
        else:
            pl.when(me_x > 0)(action)

    def place(dx, dz):
        return (place_of(me_x + dx), lax.rem(me_z + dz + count_z, count_z))

    def greet(peer):
        pl.semaphore_signal(barrier, inc=1, device_id=peer, device_id_type=MESH)

    for peer in friends:
        greet(peer)
    for dx, dz in steps:
        if dz != 0:
            reach(dx, lambda dx=dx, dz=dz: greet(place(dx, dz)))
    common = len(friends)

    def to_blocks(source, target):
        for p in range(count_y):
            rows = []
            for x in range(p * planes, (p + 1) * planes):
                slab = source[x].astype(WIDE)
                rows.append(jnp.concatenate([slab[:, z] for z in range(part_z)], axis=1))
            target[p] = (rows[0] if planes == 1 else jnp.concatenate(rows, axis=0)).astype(LOW)

    def from_blocks(source, target):
        for p in range(count_y):
            block = source[p].astype(WIDE)
            for i in range(planes):
                x = p * planes + i
                for z in range(part_z):
                    r.slab[x, :, z, :] = block[
                        i * part_y : (i + 1) * part_y, z * width : (z + 1) * width
                    ]
                target[x] = r.slab[x].astype(LOW)

    loads[0].wait()
    to_blocks(r.token_local, r.token_in)
    inner = (me_x > 0) & (me_x < count_y - 1)

    @pl.when(inner)
    def _():
        pl.semaphore_wait(barrier, common + 6)

    @pl.when(jnp.logical_not(inner))
    def _():
        pl.semaphore_wait(barrier, common + 4)

    def swap(source, target, slot, inward, first=1, last=count_y):
        copies = []
        for k in range(first, last):
            peer = lax.rem(me_y + k, count_y)
            copy = pltpu.make_async_remote_copy(
                src_ref=source.at[place_of(peer) if inward else peer],
                dst_ref=target.at[me_y if inward else me_x],
                send_sem=r.swap_send.at[slot, k],
                recv_sem=r.swap_recv.at[slot, k],
                device_id=(peer, me_z),
                device_id_type=MESH,
            )
            copy.start()
            copies.append(copy)
        return copies

    token_copies = swap(r.token_in, r.token_got, 0, True)
    loads[1].wait()
    to_blocks(r.grad_local, r.grad_in)
    grad_copies = swap(r.grad_in, r.grad_got, 1, True, 1, count_y // 2)
    r.token_got[me_y] = r.token_in[me_x]
    r.grad_got[me_y] = r.grad_in[me_x]

    def to_lines(got, target):
        for p in range(count_y):
            block = got[p].astype(WIDE)
            for line in range(lines):
                x, z = line // part_z, line % part_z
                target[pl.ds(line * length + p * part_y, part_y)] = block[
                    x * part_y : (x + 1) * part_y, z * width : (z + 1) * width
                ]

    def from_lines(source, target):
        for p in range(count_y):
            rows = [
                jnp.concatenate(
                    [
                        source[pl.ds((x * part_z + z) * length + p * part_y, part_y)]
                        for z in range(part_z)
                    ],
                    axis=1,
                )
                for x in range(planes)
            ]
            target[p] = (rows[0] if planes == 1 else jnp.concatenate(rows, axis=0)).astype(LOW)

    def conv_inside(padded, flip):
        for line in range(lines):
            plane, column = line // part_z, line % part_z
            r.conv_part[pl.ds(line * length, length)] = padded[plane + 1, column + 1].astype(
                WIDE
            ) + conv_line(padded, r.taps, plane, column, flip, True)

    def conv_rest(padded, line, flip):
        return r.conv_part[pl.ds(line * length, length)] + conv_line(
            padded, r.taps, line // part_z, line % part_z, flip, False
        )

    def halo(padded, slot):
        copies = []
        for index, (dx, dz) in enumerate(steps):
            from_x, to_x = face(dx, planes)
            from_z, to_z = face(dz, part_z)
            inside_x = pl.ds(from_x.start + 1, from_x.size)
            inside_z = pl.ds(from_z.start + 1, from_z.size)
            copies.append(
                lambda index=index, dx=dx, dz=dz, ix=inside_x, iz=inside_z, tx=to_x, tz=to_z: pltpu.make_async_remote_copy(
                    src_ref=padded.at[ix, iz],
                    dst_ref=padded.at[tx, tz],
                    send_sem=r.halo_send.at[slot, index],
                    recv_sem=r.halo_recv.at[slot, index],
                    device_id=place(dx, dz),
                    device_id_type=MESH,
                )
            )
        for index, (dx, dz) in enumerate(steps):
            reach(dx, lambda index=index: copies[index]().start())
        blank = jnp.zeros((1,) + tuple(padded.shape[1:]), padded.dtype)

        @pl.when(me_x == 0)
        def _():
            padded[0:1] = blank

        @pl.when(me_x == count_y - 1)
        def _():
            padded[planes + 1 : planes + 2] = blank

        def finish():
            for index, (dx, dz) in enumerate(steps):
                reach(dx, lambda index=index: copies[index]().wait_send())
                reach(-dx, lambda index=index: copies[index]().wait_recv())

        return finish

    me_core, me_chip = lax.rem(me_z, 2), me_z // 2

    me_even, me_far = lax.rem(me_y, 2), me_y // 2
    far = count_y // 2

    def sibling(k):
        peer = lax.rem(me_core + k, 2)
        return peer, (me_y, me_chip * 2 + peer)

    def near(k):
        even = lax.rem(me_even + k // half_z, 2)
        chip = lax.rem(me_chip + k % half_z, half_z)
        return even * half_z + chip, (me_far * 2 + even, chip * 2 + me_core)

    def distant(k):
        peer = lax.rem(me_far + k, far)
        return peer, (peer * 2 + me_even, me_z)

    groups = (
        (2, me_core, sibling),
        (2 * half_z, me_even * half_z + me_chip, near),
        (far, me_far, distant),
    )

    def send(source, target, chain, stage, k, peer):
        copy = pltpu.make_async_remote_copy(
            src_ref=source,
            dst_ref=target,
            send_sem=r.chain_send.at[chain, stage, k],
            recv_sem=r.chain_recv.at[chain, stage, k],
            device_id=peer,
            device_id_type=MESH,
        )
        copy.start()
        return copy

    def run_chain(chain):
        entry = plan.chains[chain]
        sums = r.sums
        base, size = entry.base, entry.size
        held, first = r.parts, base
        spans = []
        for level, (total, me, peer_of) in enumerate(groups):
            outgoing, incoming, result = (getattr(r, name) for name in entry.buffers[level])
            part = size // total
            outgoing[...] = held[pl.ds(first, size)].astype(LOW)
            copies = []
            for k in range(1, total):
                index, peer = peer_of(k)
                copies.append(
                    send(
                        outgoing.at[pl.ds(index * part, part)], incoming.at[k], chain, level, k, peer
                    )
                )
            yield
            summed = held[pl.ds(first + me * part, part)]
            for k, copy in enumerate(copies):
                copy.wait()
                summed = summed + incoming[k + 1].astype(WIDE)
            result[...] = summed
            held, first = result, 0
            base, size = base + me * part, part
            spans.append((base, size))
        sums[pl.ds(base, size)] = held[...].astype(LOW)
        for level in range(len(groups) - 1, -1, -1):
            total, _, peer_of = groups[level]
            span = pl.ds(*spans[level])
            copies = [
                send(sums.at[span], sums.at[span], chain, len(groups) + level, k, peer_of(k)[1])
                for k in range(1, total)
            ]
            yield
            for copy in copies:
                copy.wait()

    def leave(source, target, slot):
        copy = pltpu.make_async_copy(source, target, r.leave_sem.at[slot])
        copy.start()
        return copy

    running = []

    def launch(chain):
        if plan.chains[chain]:
            running.append(run_chain(chain))
            next(running[-1])

    def advance():
        for work in list(reversed(running)):
            if next(work, "done") == "done":
                running.remove(work)

    mask = jnp.tile(spread_mask(r.mask, length), (HEADS, 1))
    for copy in loads[2:]:
        copy.wait()
    for copy in token_copies:
        copy.wait()
    to_lines(r.token_got, r.token_wide)
    token_wide = r.token_wide[...]
    normal, inverse = norm_rows(token_wide)
    r.normal[...] = normal
    r.inverse[...] = inverse
    normed = normal.astype(LOW)
    for piece, target in enumerate((r.query, r.key, r.value)):
        target[...] = dot(normed, r.qkv_weight[:, piece * width : (piece + 1) * width]).astype(LOW)
    for line in range(lines):
        rows = pl.ds(line * length, length)
        query_vec, key_vec = r.query[rows].astype(WIDE), r.key[rows].astype(WIDE)
        query_stack = stack_heads(query_vec * unit_scale(query_vec)).astype(LOW)
        key_unit = (key_vec * unit_scale(key_vec)).astype(LOW)
        weights = mask * jnp.exp(factor * dot(query_stack, key_unit, 1, 1))
        probs = weights / jnp.sum(weights, axis=-1, keepdims=True)
        r.probs[line] = probs
        r.attended[rows] = unstack_heads(dot(probs.astype(LOW), r.value[rows])).astype(LOW)
    field = (r.token_wide[...] + dot(r.attended[...], r.out_weight[...])).astype(LOW)
    r.padded_value[1 : planes + 1, 1 : part_z + 1] = field.reshape(planes, part_z, length, width)
    finish_value = halo(r.padded_value, 0)
    grad_copies += swap(r.grad_in, r.grad_got, 1, True, count_y // 2)

    conv_inside(r.padded_value, False)
    finish_value()
    for line in range(lines):
        r.mixed[pl.ds(line * length, length)] = conv_rest(r.padded_value, line, False).astype(LOW)
    group = min(2, part_z)
    for start in range(0, lines, group):
        rows = pl.ds(start * length, group * length)
        mixed_wide = r.mixed[rows].astype(WIDE)
        normal, inverse = norm_rows(mixed_wide)
        r.normal_second[rows] = normal
        r.inverse_second[rows] = inverse
        r.normed[rows] = normal.astype(LOW)
        pre_act = dot(r.normed[rows], r.up_weight[...])
        square = pre_act * pre_act
        tangent = jnp.tanh(GELU_SLOPE * (pre_act + GELU_CUBIC * square * pre_act))
        r.hidden[rows] = (0.5 * pre_act * (1.0 + tangent)).astype(LOW)
        r.slope[rows] = 0.5 * (1.0 + tangent) + 0.5 * pre_act * (
            1.0 - tangent * tangent
        ) * GELU_SLOPE * (1.0 + 3.0 * GELU_CUBIC * square)
        r.block_wide[rows] = mixed_wide + dot(r.hidden[rows], r.down_weight[...], 1, 1)

    for copy in grad_copies:
        copy.wait()
    to_lines(r.grad_got, r.above_wide)
    for start in range(0, lines, group):
        plane, columns = start // part_z, pl.ds(start % part_z + 1, group)
        rows = pl.ds(start * length, group * length)
        grad_hidden = dot(r.above_wide[rows].astype(LOW), r.down_weight[...]).astype(LOW)
        r.grad_pre[rows] = (grad_hidden.astype(WIDE) * r.slope[rows]).astype(LOW)
        grad_normed = dot(r.grad_pre[rows], r.up_weight[...], 1, 1)
        r.padded_grad[plane + 1, columns] = (
            (
                r.above_wide[rows]
                + norm_rows_back(grad_normed, r.normal_second[rows], r.inverse_second[rows])
            )
            .astype(LOW)
            .reshape(group, length, width)
        )
    finish_grad = halo(r.padded_grad, 1)
    put_tiles(r.parts, 0, dot(r.normed[...], r.grad_pre[...], 0, 0))
    put_tiles(r.parts, plan.tiles, dot(r.above_wide[...].astype(LOW), r.hidden[...], 0, 0))
    launch(0)

    r.tap_sums[...] = jnp.zeros_like(r.tap_sums)
    for line in range(lines):
        plane, column = line // part_z, line % part_z
        centre = r.padded_grad[plane + 1, column + 1].astype(WIDE)
        shifted = (shift_rows(centre, -1), centre, shift_rows(centre, 1))
        for a in range(3):
            for d in range(3):
                window = r.padded_value[plane + a, column + d].astype(WIDE)
                for b in range(3):
                    product = (shifted[b] * window).reshape(length // 8, 8, width)
                    r.tap_sums[(a * 3 + b) * 3 + d] += jnp.sum(product, axis=0)
    r.tap_flat[...] = jnp.zeros_like(r.tap_flat)
    r.tap_flat[:27, :width] = jnp.sum(r.tap_sums[...], axis=1)
    put_tiles(r.parts, 2 * plan.tiles, r.tap_flat[...])
    if plan.pad:
        r.parts[plan.used :] = jnp.zeros((plan.pad, 16, 128), WIDE)
    from_lines(r.block_wide, r.block_sent)
    conv_inside(r.padded_grad, True)
    advance()
    finish_grad()
    block_copies = swap(r.block_sent, r.block_got, 2, False)
    r.block_got[me_x] = r.block_sent[me_y]

    for line in range(lines):
        r.grad_value[pl.ds(line * length, length)] = conv_rest(r.padded_grad, line, True).astype(LOW)
    r.above[...] = dot(r.grad_value[...], r.out_weight[...], 1, 1).astype(LOW)
    r.joint[:, 3 * width :] = dot(r.attended[...], r.grad_value[...], 0, 0)
    for line in range(lines):
        rows = pl.ds(line * length, length)
        query_vec, key_vec = r.query[rows].astype(WIDE), r.key[rows].astype(WIDE)
        query_scale, key_scale = unit_scale(query_vec), unit_scale(key_vec)
        query_stack = stack_heads(query_vec * query_scale).astype(LOW)
        key_unit = (key_vec * key_scale).astype(LOW)
        probs = r.probs[line]
        grad_stack = stack_heads(r.above[rows].astype(WIDE)).astype(LOW)
        grad_probs = dot(grad_stack, r.value[rows], 1, 1)
        grad_scores = probs * (grad_probs - jnp.sum(grad_probs * probs, axis=-1, keepdims=True))
        grad_low = (factor * grad_scores).astype(LOW)
        r.grad_v[rows] = dot(probs.astype(LOW), grad_stack, 0, 0).astype(LOW)
        grad_qunit = unstack_heads(dot(grad_low, key_unit))
        grad_kunit = dot(grad_low, query_stack, 0, 0)
        r.grad_q[rows] = unit_back(grad_qunit, query_vec, query_scale).astype(LOW)
        r.grad_k[rows] = unit_back(grad_kunit, key_vec, key_scale).astype(LOW)
    advance()
    normal = r.normal[...]
    normed = normal.astype(LOW)
    pieces = [
        (slice(piece * width, (piece + 1) * width), grad)
        for piece, grad in enumerate((r.grad_q, r.grad_k, r.grad_v))
    ]
    for part, grad in pieces:
        r.joint[:, part] = dot(normed, grad[...], 0, 0)
    put_tiles(r.parts, 2 * plan.tiles + plan.tap_tiles, r.joint[...])
    launch(1)
    grad_normed = 0.0
    for part, grad in pieces:
        grad_normed = grad_normed + dot(grad[...], r.qkv_weight[:, part], 1, 1)
    upstream = grad_normed.astype(LOW).astype(WIDE)
    r.block_wide[...] = r.grad_value[...].astype(WIDE) + norm_rows_back(
        upstream, normal, r.inverse[...]
    )
    from_lines(r.block_wide, r.token_sent)
    token_copies = swap(r.token_sent, r.token_back, 3, False)
    r.token_back[me_x] = r.token_sent[me_y]
    advance()
    for copy in block_copies:
        copy.wait()
    from_blocks(r.block_got, r.block_local)
    leaves = [leave(r.block_local, r.block_out, 0)]
    advance()
    advance()
    for copy in token_copies:
        copy.wait()
    from_blocks(r.token_back, r.token_local)
    leaves.append(leave(r.token_local, r.token_out, 1))
    while len(running) > 1:
        advance()
    cut = plan.chains[1].base
    if cut:
        leaves.append(leave(r.sums.at[:cut], r.sums_out.at[:cut], 2))
    while running:
        advance()
    leaves.append(leave(r.sums.at[cut:], r.sums_out.at[cut:], 3))
    for copy in leaves:
        copy.wait()


def make_plan(count_y, count_z, extents, hidden_width):
    planes, part_y, part_z, width = extents
    devices = count_y * count_z
    rows = width // 16
    tiles = rows * (hidden_width // 128)
    tap_tiles = 4
    used = 2 * tiles + tap_tiles + rows * (4 * width // 128)
    whole = -(-used // devices) * devices
    chains, buffers = [], []
    cut = 2 * tiles // devices * devices
    sizes = (2, count_z // 2 * 2, count_y // 2)
    for index, (base, size) in enumerate(((0, cut), (cut, whole - cut))):
        names, left = [], size
        for level, total in enumerate(sizes):
            part = left // total
            names.append(["chain%d_%s%d" % (index, kind, level) for kind in ("out", "in", "sum")])
            shapes = ((left, 16, 128), (total, part, 16, 128), (part, 16, 128))
            buffers += list(zip(names[-1], shapes, (LOW, LOW, WIDE))) if size else []
            left = part
        chains.append(types.SimpleNamespace(base=base, size=size, buffers=names) if size else None)
    return types.SimpleNamespace(
        count_y=count_y, count_z=count_z, planes=planes, part_y=part_y, part_z=part_z, width=width,
        hidden=hidden_width, tiles=tiles, tap_tiles=tap_tiles, used=used, whole=whole,
        pad=whole - used, chains=chains, buffers=buffers, most=max(sizes), levels=len(sizes),
    )


def run_block(plan, tokens, upstream, weights, mask):
    count_y, width, hidden = plan.count_y, plan.width, plan.hidden
    lines, length = plan.planes * plan.part_z, plan.part_y * plan.count_y
    count = lines * length
    blocks = (count_y, plan.planes * plan.part_y, plan.part_z * width)
    padded = (plan.planes + 2, plan.part_z + 2, length, width)

    def low(*shape):
        return pltpu.VMEM(shape, LOW)

    def wide(*shape):
        return pltpu.VMEM(shape, WIDE)

    slots = (len(plan.chains), 2 * plan.levels, plan.most)
    scratch = {
        "swap_send": pltpu.SemaphoreType.DMA((4, count_y)),
        "swap_recv": pltpu.SemaphoreType.DMA((4, count_y)),
        "halo_send": pltpu.SemaphoreType.DMA((2, 8)),
        "halo_recv": pltpu.SemaphoreType.DMA((2, 8)),
        "chain_send": pltpu.SemaphoreType.DMA(slots),
        "chain_recv": pltpu.SemaphoreType.DMA(slots),
        "load_sem": pltpu.SemaphoreType.DMA((2 + len(weights),)),
        "leave_sem": pltpu.SemaphoreType.DMA((4,)),
        "qkv_weight": low(width, 3 * width),
        "out_weight": low(width, width),
        "taps": wide(3, 3, 3, width),
        "up_weight": low(width, hidden),
        "down_weight": low(width, hidden),
        "sums": low(plan.whole, 16, 128),
        "token_local": low(*tokens.shape),
        "grad_local": low(*tokens.shape),
        "block_local": low(*tokens.shape),
        "slab": wide(*tokens.shape),
        "token_in": low(*blocks),
        "grad_in": low(*blocks),
        "block_got": low(*blocks),
        "token_back": low(*blocks),
        "token_got": low(*blocks),
        "grad_got": low(*blocks),
        "block_sent": low(*blocks),
        "token_sent": low(*blocks),
        "token_wide": wide(count, width),
        "above_wide": wide(count, width),
        "block_wide": wide(count, width),
        "normal": wide(count, width),
        "inverse": wide(count, 1),
        "normal_second": wide(count, width),
        "inverse_second": wide(count, 1),
        "slope": wide(count, hidden),
        "conv_part": wide(count, width),
        "query": low(count, width),
        "key": low(count, width),
        "value": low(count, width),
        "attended": low(count, width),
        "probs": wide(lines, HEADS * length, length),
        "padded_value": low(*padded),
        "padded_grad": low(*padded),
        "mixed": low(count, width),
        "normed": low(count, width),
        "hidden": low(count, hidden),
        "grad_pre": low(count, hidden),
        "tap_sums": wide(27, 8, width),
        "tap_flat": wide(32, 256),
        "grad_value": low(count, width),
        "above": low(count, width),
        "grad_q": low(count, width),
        "grad_k": low(count, width),
        "grad_v": low(count, width),
        "joint": wide(width, 4 * width),
        "parts": wide(plan.whole, 16, 128),
    }
    for name, shape, kind in plan.buffers:
        scratch[name] = pltpu.VMEM(shape, kind)
    names = ["token_slab", "grad_slab", "qkv_hbm", "out_hbm", "taps_hbm", "up_hbm", "down_hbm", "mask"]
    outs = {
        "block_out": jax.ShapeDtypeStruct(tokens.shape, LOW),
        "token_out": jax.ShapeDtypeStruct(tokens.shape, LOW),
        "sums_out": jax.ShapeDtypeStruct((plan.whole, 16, 128), LOW),
    }
    plan.names = names + list(outs) + list(scratch)
    return pl.pallas_call(
        functools.partial(block_kernel, plan),
        out_shape=tuple(outs.values()),
        in_specs=[ANY, ANY] + [ANY] * len(weights) + [SMEM],
        out_specs=(ANY,) * len(outs),
        scratch_shapes=list(scratch.values()),
        compiler_params=pltpu.CompilerParams(
            collective_id=0, has_side_effects=True, vmem_limit_bytes=60 * 1024 * 1024
        ),
        name="block",
    )(tokens, upstream, *weights, mask)


def finish_kernel(plan, factor, sums_in, block_in, token_in, *refs):
    (block_out, token_out, qkv_out, out_out, kernel_out, up_out, down_out) = refs[:7]
    sums, block, token, qkv, out, kernel, up, down, joint, load_sem, sem = refs[7:]
    rows = plan.width // 16
    copies = []

    def leave(source, target):
        copies.append(pltpu.make_async_copy(source, target, sem.at[len(copies)]))
        copies[-1].start()

    def tile(first):
        return sums[first : first + rows].astype(WIDE).reshape(plan.width, 128) * factor

    loads = []
    for source, target in (
        (sums_in.at[: plan.tiles], sums.at[: plan.tiles]),
        (sums_in.at[plan.tiles :], sums.at[plan.tiles :]),
        (block_in, block),
        (token_in, token),
    ):
        copy = pltpu.make_async_copy(source, target, load_sem.at[len(loads)])
        copy.start()
        loads.append(copy)
    taps_at = 2 * plan.tiles
    joint_at = taps_at + plan.tap_tiles
    for base, target, result, load in (
        (0, up, up_out, loads[0]),
        (plan.tiles, down, down_out, loads[1]),
    ):
        load.wait()
        for index in range(plan.hidden // 128):
            target[:, index * 128 : (index + 1) * 128] = tile(base + index * rows)
        leave(target, result)
    for source, target, load in ((block, block_out, loads[2]), (token, token_out, loads[3])):
        load.wait()
        leave(source, target)
    for index in range(4 * plan.width // 128):
        joint[:, index * 128 : (index + 1) * 128] = tile(joint_at + index * rows)
    qkv[...] = joint[:, : 3 * plan.width]
    leave(qkv, qkv_out)
    out[...] = joint[:, 3 * plan.width :]
    leave(out, out_out)
    taps = sums[taps_at:joint_at].astype(WIDE) * factor
    flat = jnp.concatenate([taps[:2].reshape(32, 128), taps[2:].reshape(32, 128)], axis=1)
    for a in range(3):
        for b in range(3):
            first = (a * 3 + b) * 3
            kernel[a, b] = flat[first : first + 3, : plan.width]
    leave(kernel, kernel_out)
    for copy in copies:
        copy.wait()


def finish(plan, factor, sums, block_out, token_out):
    width, hidden = plan.width, plan.hidden
    shapes = ((width, 3 * width), (width, width), (3, 3, 3, width), (width, hidden), (width, hidden))
    outs = [jax.ShapeDtypeStruct(block_out.shape, LOW)] * 2
    outs += [jax.ShapeDtypeStruct(shape, WIDE) for shape in shapes]
    return pl.pallas_call(
        functools.partial(finish_kernel, plan, factor),
        out_shape=tuple(outs),
        in_specs=[ANY] * 3,
        out_specs=(ANY,) * len(outs),
        scratch_shapes=[pltpu.VMEM(x.shape, LOW) for x in (sums, block_out, token_out)]
        + [pltpu.VMEM(shape, WIDE) for shape in shapes]
        + [
            pltpu.VMEM((width, 4 * width), WIDE),
            pltpu.SemaphoreType.DMA((4,)),
            pltpu.SemaphoreType.DMA((len(outs),)),
        ],
        compiler_params=pltpu.CompilerParams(vmem_limit_bytes=60 * 1024 * 1024),
        name="finish",
    )(sums, block_out, token_out)


def local(tokens, qkv_weight, out_weight, conv_kernel, up_weight, down_weight, band_mask, grad_out):
    count_y, count_z = lax.axis_size("gy"), lax.axis_size("gz")
    extent_x, part_y, part_z, width = tokens.shape
    planes = extent_x // count_y
    plan = make_plan(count_y, count_z, (planes, part_y, part_z, width), up_weight.shape[1])
    weights = (qkv_weight, out_weight, conv_kernel, up_weight, down_weight.T)
    block_out, token_gradient, sums = run_block(
        plan, tokens, grad_out, weights, band_mask
    )
    factor = 1.0 / math.sqrt(extent_x * part_y * count_y * part_z * count_z)
    block_out, token_gradient, qkv_sum, out_sum, kernel_sum, up_sum, down_sum = finish(
        plan, factor, sums, block_out, token_gradient
    )
    return (
        block_out,
        token_gradient,
        qkv_sum,
        out_sum,
        kernel_sum,
        up_sum,
        down_sum.T,
    )


def solution(mesh):
    placed = (P(None, "gy", "gz", None), P(), P(), P(), P(), P(), P(), P(None, "gy", "gz", None))
    return jax.shard_map(
        local,
        mesh=mesh,
        in_specs=placed,
        out_specs=(P(None, "gy", "gz", None), P(None, "gy", "gz", None), P(), P(), P(), P(), P()),
        check_vma=False,
    )
```

```python
import functools
import math
import types

import jax
import jax.numpy as jnp
from jax import lax
from jax.experimental import pallas as pl
from jax.experimental.pallas import tpu as pltpu
from jax.sharding import PartitionSpec as P

HEADS = 6
BLOCK = 16


NORM_EPS = 1e-05
UNIT_EPS = 1e-06
GELU_SLOPE = 0.7978845608028654
GELU_CUBIC = 0.044715

MESH = pl.DeviceIdType.MESH
SMEM = pl.BlockSpec(memory_space=pltpu.SMEM)
ANY = pl.BlockSpec(memory_space=pl.ANY)
LOW = jnp.bfloat16
WIDE = jnp.float32


def norm_rows(values):
    centred = values - jnp.mean(values, axis=-1, keepdims=True)
    inverse = lax.rsqrt(jnp.mean(centred * centred, axis=-1, keepdims=True) + NORM_EPS)
    return (centred * inverse, inverse)


def norm_rows_back(upstream, normal, inverse):
    return inverse * (
        upstream
        - jnp.mean(upstream, axis=-1, keepdims=True)
        - normal * jnp.mean(upstream * normal, axis=-1, keepdims=True)
    )


def unit_scale(values):
    return lax.rsqrt(jnp.mean(values * values, axis=-1, keepdims=True) + UNIT_EPS)


def unit_back(upstream, values, scaling):
    return scaling * upstream - scaling * scaling * scaling * values * jnp.mean(
        upstream * values, axis=-1, keepdims=True
    )


def place_of(index):
    return index + (1 - 2 * lax.rem(index, 2)) * lax.rem(index // 2, 2)


def dot(left, right, left_axis=1, right_axis=0):
    return lax.dot_general(
        left, right, (((left_axis,), (right_axis,)), ((), ())), preferred_element_type=WIDE
    )


def stack_heads(values):
    width = values.shape[1]
    head_of = lax.broadcasted_iota(jnp.int32, (1, width), 1) // (width // HEADS)
    return jnp.concatenate([jnp.where(head_of == h, values, 0.0) for h in range(HEADS)], axis=0)


def unstack_heads(stacked):
    rows, width = stacked.shape[0] // HEADS, stacked.shape[1]
    head_of = lax.broadcasted_iota(jnp.int32, (1, width), 1) // (width // HEADS)
    joined = stacked[:rows]
    for h in range(1, HEADS):
        joined = jnp.where(head_of == h, stacked[h * rows : (h + 1) * rows], joined)
    return joined


def shift_rows(values, step):
    return pltpu.roll(values, step % values.shape[0], 0)


def face(step, extent):
    return {
        0: (pl.ds(0, extent), pl.ds(1, extent)),
        1: (pl.ds(extent - 1, 1), pl.ds(0, 1)),
        -1: (pl.ds(0, 1), pl.ds(extent + 1, 1)),
    }[step]


def conv_line(padded, taps, plane, column, flip, inside):
    by_shift = [None, None, None]
    for a in range(3):
        for d in range(3):
            x, z = plane + a, column + d
            here = 0 < x < padded.shape[0] - 1 and 0 < z < padded.shape[1] - 1
            if here != inside:
                continue
            window = padded[x, z].astype(WIDE)
            for b in range(3):
                tap = taps[2 - a, 2 - b, 2 - d : 3 - d] if flip else taps[a, b, d : d + 1]
                term = tap * window
                by_shift[b] = term if by_shift[b] is None else by_shift[b] + term
    if by_shift[0] is None:
        return 0.0
    return shift_rows(by_shift[0], 1) + by_shift[1] + shift_rows(by_shift[2], -1)


def put_tiles(target, base, matrix):
    rows = matrix.shape[0] // 16
    for column in range(matrix.shape[1] // 128):
        target[base + column * rows : base + (column + 1) * rows] = matrix[
            :, column * 128 : (column + 1) * 128
        ].reshape(rows, 16, 128)


def spread_mask(mask, length):
    blocks = length // BLOCK
    column = lax.broadcasted_iota(jnp.int32, (BLOCK, length), 1) // BLOCK
    rows = []
    for i in range(blocks):
        row = jnp.zeros((BLOCK, length), jnp.int32)
        for j in range(blocks):
            row = jnp.where(column == j, mask[i, j], row)
        rows.append(row)
    return jnp.concatenate(rows, axis=0).astype(WIDE)


def block_kernel(plan, *refs):
    r = types.SimpleNamespace(**dict(zip(plan.names, refs)))
    count_y, count_z = plan.count_y, plan.count_z
    planes, part_y, part_z, width = plan.planes, plan.part_y, plan.part_z, plan.width
    lines, length = planes * part_z, part_y * count_y
    count = lines * length
    factor = 2.0 / math.sqrt(width // HEADS)
    me_y, me_z = lax.axis_index("gy"), lax.axis_index("gz")
    me_x = place_of(me_y)

    moved = (
        (r.token_slab, r.token_local),
        (r.grad_slab, r.grad_local),
        (r.qkv_hbm, r.qkv_weight),
        (r.out_hbm, r.out_weight),
        (r.taps_hbm, r.taps),
        (r.up_hbm, r.up_weight),
        (r.down_hbm, r.down_weight),
    )
    loads = [
        pltpu.make_async_copy(source, target, r.load_sem.at[index])
        for index, (source, target) in enumerate(moved)
    ]
    for copy in loads:
        copy.start()

    steps = [(-1, 0), (1, 0), (0, -1), (0, 1), (-1, -1), (-1, 1), (1, -1), (1, 1)]
    half_z = max(1, count_z // 2)
    flip = me_y + 1 - 2 * lax.rem(me_y, 2)
    friends = [(lax.rem(me_y + k, count_y), me_z) for k in range(1, count_y)]
    friends += [(me_y, me_z + 1 - 2 * lax.rem(me_z, 2))]
    friends += [
        (peer, lax.rem(me_z + 2 * k, count_z)) for k in range(1, half_z) for peer in (me_y, flip)
    ]
    barrier = pltpu.get_barrier_semaphore()

    def reach(dx, action):
        if dx == 0:
            action()
        elif dx == 1:
            pl.when(me_x < count_y - 1)(action)
        else:
            pl.when(me_x > 0)(action)

    def place(dx, dz):
        return (place_of(me_x + dx), lax.rem(me_z + dz + count_z, count_z))

    def greet(peer):
        pl.semaphore_signal(barrier, inc=1, device_id=peer, device_id_type=MESH)

    for peer in friends:
        greet(peer)
    for dx, dz in steps:
        if dz != 0:
            reach(dx, lambda dx=dx, dz=dz: greet(place(dx, dz)))
    common = len(friends)

    def to_blocks(source, target):
        for p in range(count_y):
            rows = []
            for x in range(p * planes, (p + 1) * planes):
                slab = source[x].astype(WIDE)
                rows.append(jnp.concatenate([slab[:, z] for z in range(part_z)], axis=1))
            target[p] = (rows[0] if planes == 1 else jnp.concatenate(rows, axis=0)).astype(LOW)

    def from_blocks(source, target):
        for p in range(count_y):
            block = source[p].astype(WIDE)
            for i in range(planes):
                x = p * planes + i
                for z in range(part_z):
                    r.slab[x, :, z, :] = block[
                        i * part_y : (i + 1) * part_y, z * width : (z + 1) * width
                    ]
                target[x] = r.slab[x].astype(LOW)

    loads[0].wait()
    to_blocks(r.token_local, r.token_in)
    inner = (me_x > 0) & (me_x < count_y - 1)

    @pl.when(inner)
    def _():
        pl.semaphore_wait(barrier, common + 6)

    @pl.when(jnp.logical_not(inner))
    def _():
        pl.semaphore_wait(barrier, common + 4)

    def swap(source, target, slot, inward, first=1, last=count_y):
        copies = []
        for k in sorted(range(first, last), key=lambda k: abs(2 * k - count_y)):
            peer = lax.rem(me_y + k, count_y)
            copy = pltpu.make_async_remote_copy(
                src_ref=source.at[place_of(peer) if inward else peer],
                dst_ref=target.at[me_y if inward else me_x],
                send_sem=r.swap_send.at[slot, k],
                recv_sem=r.swap_recv.at[slot, k],
                device_id=(peer, me_z),
                device_id_type=MESH,
            )
            copy.start()
            copies.append(copy)
        return copies

    token_copies = swap(r.token_in, r.token_got, 0, True)
    loads[1].wait()
    to_blocks(r.grad_local, r.grad_in)
    grad_copies = swap(r.grad_in, r.grad_got, 1, True, 1, count_y // 2)
    r.token_got[me_y] = r.token_in[me_x]
    r.grad_got[me_y] = r.grad_in[me_x]

    def to_lines(got, target):
        for p in range(count_y):
            block = got[p].astype(WIDE)
            for line in range(lines):
                x, z = line // part_z, line % part_z
                target[pl.ds(line * length + p * part_y, part_y)] = block[
                    x * part_y : (x + 1) * part_y, z * width : (z + 1) * width
                ]

    def from_lines(source, target):
        for p in range(count_y):
            rows = [
                jnp.concatenate(
                    [
                        source[pl.ds((x * part_z + z) * length + p * part_y, part_y)]
                        for z in range(part_z)
                    ],
                    axis=1,
                )
                for x in range(planes)
            ]
            target[p] = (rows[0] if planes == 1 else jnp.concatenate(rows, axis=0)).astype(LOW)

    def conv_inside(padded, flip):
        for line in range(lines):
            plane, column = line // part_z, line % part_z
            r.conv_part[pl.ds(line * length, length)] = padded[plane + 1, column + 1].astype(
                WIDE
            ) + conv_line(padded, r.taps, plane, column, flip, True)

    def conv_rest(padded, line, flip):
        return r.conv_part[pl.ds(line * length, length)] + conv_line(
            padded, r.taps, line // part_z, line % part_z, flip, False
        )

    def halo(padded, slot):
        copies = []
        for index, (dx, dz) in enumerate(steps):
            from_x, to_x = face(dx, planes)
            from_z, to_z = face(dz, part_z)
            inside_x = pl.ds(from_x.start + 1, from_x.size)
            inside_z = pl.ds(from_z.start + 1, from_z.size)
            copies.append(
                lambda index=index, dx=dx, dz=dz, ix=inside_x, iz=inside_z, tx=to_x, tz=to_z: pltpu.make_async_remote_copy(
                    src_ref=padded.at[ix, iz],
                    dst_ref=padded.at[tx, tz],
                    send_sem=r.halo_send.at[slot, index],
                    recv_sem=r.halo_recv.at[slot, index],
                    device_id=place(dx, dz),
                    device_id_type=MESH,
                )
            )
        for index, (dx, dz) in enumerate(steps):
            reach(dx, lambda index=index: copies[index]().start())
        blank = jnp.zeros((1,) + tuple(padded.shape[1:]), padded.dtype)

        @pl.when(me_x == 0)
        def _():
            padded[0:1] = blank

        @pl.when(me_x == count_y - 1)
        def _():
            padded[planes + 1 : planes + 2] = blank

        def finish():
            for index, (dx, dz) in enumerate(steps):
                reach(dx, lambda index=index: copies[index]().wait_send())
                reach(-dx, lambda index=index: copies[index]().wait_recv())

        return finish

    me_core, me_chip = lax.rem(me_z, 2), me_z // 2

    me_even, me_far = lax.rem(me_y, 2), me_y // 2
    far = count_y // 2

    def sibling(k):
        peer = lax.rem(me_core + k, 2)
        return peer, (me_y, me_chip * 2 + peer)

    def near(k):
        even = lax.rem(me_even + k // half_z, 2)
        chip = lax.rem(me_chip + k % half_z, half_z)
        return even * half_z + chip, (me_far * 2 + even, chip * 2 + me_core)

    def distant(k):
        peer = lax.rem(me_far + k, far)
        return peer, (peer * 2 + me_even, me_z)

    groups = (
        (2, me_core, sibling),
        (2 * half_z, me_even * half_z + me_chip, near),
        (far, me_far, distant),
    )

    def send(source, target, chain, stage, k, peer):
        copy = pltpu.make_async_remote_copy(
            src_ref=source,
            dst_ref=target,
            send_sem=r.chain_send.at[chain, stage, k],
            recv_sem=r.chain_recv.at[chain, stage, k],
            device_id=peer,
            device_id_type=MESH,
        )
        copy.start()
        return copy

    def run_chain(chain):
        entry = plan.chains[chain]
        sums = r.sums
        base, size = entry.base, entry.size
        held, first = r.parts, base
        spans = []
        for level, (total, me, peer_of) in enumerate(groups):
            outgoing, incoming, result = (getattr(r, name) for name in entry.buffers[level])
            part = size // total
            outgoing[...] = held[pl.ds(first, size)].astype(LOW)
            copies = []
            for k in range(1, total):
                index, peer = peer_of(k)
                copies.append(
                    send(
                        outgoing.at[pl.ds(index * part, part)], incoming.at[k], chain, level, k, peer
                    )
                )
            yield
            summed = held[pl.ds(first + me * part, part)]
            for k, copy in enumerate(copies):
                copy.wait()
                summed = summed + incoming[k + 1].astype(WIDE)
            result[...] = summed
            held, first = result, 0
            base, size = base + me * part, part
            spans.append((base, size))
        sums[pl.ds(base, size)] = held[...].astype(LOW)
        for level in range(len(groups) - 1, -1, -1):
            total, _, peer_of = groups[level]
            span = pl.ds(*spans[level])
            copies = [
                send(sums.at[span], sums.at[span], chain, len(groups) + level, k, peer_of(k)[1])
                for k in range(1, total)
            ]
            yield
            for copy in copies:
                copy.wait()

    def leave(source, target, slot):
        copy = pltpu.make_async_copy(source, target, r.leave_sem.at[slot])
        copy.start()
        return copy

    running = []

    def launch(chain):
        if plan.chains[chain]:
            running.append(run_chain(chain))
            next(running[-1])

    def advance():
        for work in list(reversed(running)):
            if next(work, "done") == "done":
                running.remove(work)

    mask = jnp.tile(spread_mask(r.mask, length), (HEADS, 1))
    for copy in loads[2:]:
        copy.wait()
    for copy in token_copies:
        copy.wait()
    to_lines(r.token_got, r.token_wide)
    token_wide = r.token_wide[...]
    normal, inverse = norm_rows(token_wide)
    r.normal[...] = normal
    r.inverse[...] = inverse
    normed = normal.astype(LOW)
    for piece, target in enumerate((r.query, r.key, r.value)):
        target[...] = dot(normed, r.qkv_weight[:, piece * width : (piece + 1) * width]).astype(LOW)
    for line in range(lines):
        rows = pl.ds(line * length, length)
        query_vec, key_vec = r.query[rows].astype(WIDE), r.key[rows].astype(WIDE)
        query_scale, key_scale = unit_scale(query_vec), unit_scale(key_vec)
        query_stack = stack_heads(query_vec * query_scale).astype(LOW)
        key_unit = (key_vec * key_scale).astype(LOW)
        r.query_scale[rows], r.key_scale[rows] = query_scale, key_scale
        r.query_stack[line], r.key_unit[rows] = query_stack, key_unit
        weights = mask * jnp.exp(factor * dot(query_stack, key_unit, 1, 1))
        probs = weights / jnp.sum(weights, axis=-1, keepdims=True)
        r.probs[line] = probs
        r.attended[rows] = unstack_heads(dot(probs.astype(LOW), r.value[rows])).astype(LOW)
    field = (r.token_wide[...] + dot(r.attended[...], r.out_weight[...])).astype(LOW)
    r.padded_value[1 : planes + 1, 1 : part_z + 1] = field.reshape(planes, part_z, length, width)
    finish_value = halo(r.padded_value, 0)
    grad_copies += swap(r.grad_in, r.grad_got, 1, True, count_y // 2)

    conv_inside(r.padded_value, False)
    finish_value()
    for line in range(lines):
        r.mixed[pl.ds(line * length, length)] = conv_rest(r.padded_value, line, False).astype(LOW)
    group = min(2, part_z)
    for start in range(0, lines, group):
        rows = pl.ds(start * length, group * length)
        mixed_wide = r.mixed[rows].astype(WIDE)
        normal, inverse = norm_rows(mixed_wide)
        r.normal_second[rows] = normal
        r.inverse_second[rows] = inverse
        r.normed[rows] = normal.astype(LOW)
        pre_act = dot(r.normed[rows], r.up_weight[...])
        square = pre_act * pre_act
        tangent = jnp.tanh(GELU_SLOPE * (pre_act + GELU_CUBIC * square * pre_act))
        r.hidden[rows] = (0.5 * pre_act * (1.0 + tangent)).astype(LOW)
        r.slope[rows] = 0.5 * (1.0 + tangent) + 0.5 * pre_act * (
            1.0 - tangent * tangent
        ) * GELU_SLOPE * (1.0 + 3.0 * GELU_CUBIC * square)
        r.block_wide[rows] = mixed_wide + dot(r.hidden[rows], r.down_weight[...], 1, 1)

    for copy in grad_copies:
        copy.wait()
    to_lines(r.grad_got, r.above_wide)
    for start in range(0, lines, group):
        plane, columns = start // part_z, pl.ds(start % part_z + 1, group)
        rows = pl.ds(start * length, group * length)
        grad_hidden = dot(r.above_wide[rows].astype(LOW), r.down_weight[...]).astype(LOW)
        r.grad_pre[rows] = (grad_hidden.astype(WIDE) * r.slope[rows]).astype(LOW)
        grad_normed = dot(r.grad_pre[rows], r.up_weight[...], 1, 1)
        r.padded_grad[plane + 1, columns] = (
            (
                r.above_wide[rows]
                + norm_rows_back(grad_normed, r.normal_second[rows], r.inverse_second[rows])
            )
            .astype(LOW)
            .reshape(group, length, width)
        )
    finish_grad = halo(r.padded_grad, 1)
    put_tiles(r.parts, 0, dot(r.normed[...], r.grad_pre[...], 0, 0))
    put_tiles(r.parts, plan.tiles, dot(r.above_wide[...].astype(LOW), r.hidden[...], 0, 0))
    launch(0)

    r.tap_sums[...] = jnp.zeros_like(r.tap_sums)
    for line in range(lines):
        plane, column = line // part_z, line % part_z
        centre = r.padded_grad[plane + 1, column + 1].astype(WIDE)
        shifted = (shift_rows(centre, -1), centre, shift_rows(centre, 1))
        for a in range(3):
            for d in range(3):
                window = r.padded_value[plane + a, column + d].astype(WIDE)
                for b in range(3):
                    product = (shifted[b] * window).reshape(length // 8, 8, width)
                    r.tap_sums[(a * 3 + b) * 3 + d] += jnp.sum(product, axis=0)
    r.tap_flat[...] = jnp.zeros_like(r.tap_flat)
    r.tap_flat[:27, :width] = jnp.sum(r.tap_sums[...], axis=1)
    put_tiles(r.parts, 2 * plan.tiles, r.tap_flat[...])
    if plan.pad:
        r.parts[plan.used :] = jnp.zeros((plan.pad, 16, 128), WIDE)
    from_lines(r.block_wide, r.block_sent)
    conv_inside(r.padded_grad, True)
    advance()
    finish_grad()
    block_copies = swap(r.block_sent, r.block_got, 2, False)
    r.block_got[me_x] = r.block_sent[me_y]

    for line in range(lines):
        r.grad_value[pl.ds(line * length, length)] = conv_rest(r.padded_grad, line, True).astype(LOW)
    r.above[...] = dot(r.grad_value[...], r.out_weight[...], 1, 1).astype(LOW)
    r.joint[:, 3 * width :] = dot(r.attended[...], r.grad_value[...], 0, 0)
    for line in range(lines):
        rows = pl.ds(line * length, length)
        query_vec, key_vec = r.query[rows].astype(WIDE), r.key[rows].astype(WIDE)
        query_scale, key_scale = r.query_scale[rows], r.key_scale[rows]
        query_stack, key_unit = r.query_stack[line], r.key_unit[rows]
        probs = r.probs[line]
        grad_stack = stack_heads(r.above[rows].astype(WIDE)).astype(LOW)
        grad_probs = dot(grad_stack, r.value[rows], 1, 1)
        grad_scores = probs * (grad_probs - jnp.sum(grad_probs * probs, axis=-1, keepdims=True))
        grad_low = (factor * grad_scores).astype(LOW)
        r.grad_v[rows] = dot(probs.astype(LOW), grad_stack, 0, 0).astype(LOW)
        grad_qunit = unstack_heads(dot(grad_low, key_unit))
        grad_kunit = dot(grad_low, query_stack, 0, 0)
        r.grad_q[rows] = unit_back(grad_qunit, query_vec, query_scale).astype(LOW)
        r.grad_k[rows] = unit_back(grad_kunit, key_vec, key_scale).astype(LOW)
    advance()
    normal = r.normal[...]
    normed = normal.astype(LOW)
    pieces = [
        (slice(piece * width, (piece + 1) * width), grad)
        for piece, grad in enumerate((r.grad_q, r.grad_k, r.grad_v))
    ]
    for part, grad in pieces:
        r.joint[:, part] = dot(normed, grad[...], 0, 0)
    put_tiles(r.parts, 2 * plan.tiles + plan.tap_tiles, r.joint[...])
    launch(1)
    grad_normed = 0.0
    for part, grad in pieces:
        grad_normed = grad_normed + dot(grad[...], r.qkv_weight[:, part], 1, 1)
    upstream = grad_normed.astype(LOW).astype(WIDE)
    r.block_wide[...] = r.grad_value[...].astype(WIDE) + norm_rows_back(
        upstream, normal, r.inverse[...]
    )
    from_lines(r.block_wide, r.token_sent)
    token_copies = swap(r.token_sent, r.token_back, 3, False)
    r.token_back[me_x] = r.token_sent[me_y]
    advance()
    for copy in block_copies:
        copy.wait()
    from_blocks(r.block_got, r.block_local)
    leaves = [leave(r.block_local, r.block_out, 0)]
    advance()
    advance()
    for copy in token_copies:
        copy.wait()
    from_blocks(r.token_back, r.token_local)
    leaves.append(leave(r.token_local, r.token_out, 1))
    while len(running) > 1:
        advance()
    cut = plan.chains[1].base
    if cut:
        leaves.append(leave(r.sums.at[:cut], r.sums_out.at[:cut], 2))
    while running:
        advance()
    leaves.append(leave(r.sums.at[cut:], r.sums_out.at[cut:], 3))
    for copy in leaves:
        copy.wait()


def make_plan(count_y, count_z, extents, hidden_width):
    planes, part_y, part_z, width = extents
    devices = count_y * count_z
    rows = width // 16
    tiles = rows * (hidden_width // 128)
    tap_tiles = 4
    used = 2 * tiles + tap_tiles + rows * (4 * width // 128)
    whole = -(-used // devices) * devices
    chains, buffers = [], []
    cut = 2 * tiles // devices * devices
    sizes = (2, count_z // 2 * 2, count_y // 2)
    for index, (base, size) in enumerate(((0, cut), (cut, whole - cut))):
        names, left = [], size
        for level, total in enumerate(sizes):
            part = left // total
            names.append(["chain%d_%s%d" % (index, kind, level) for kind in ("out", "in", "sum")])
            shapes = ((left, 16, 128), (total, part, 16, 128), (part, 16, 128))
            buffers += list(zip(names[-1], shapes, (LOW, LOW, WIDE))) if size else []
            left = part
        chains.append(types.SimpleNamespace(base=base, size=size, buffers=names) if size else None)
    return types.SimpleNamespace(
        count_y=count_y, count_z=count_z, planes=planes, part_y=part_y, part_z=part_z, width=width,
        hidden=hidden_width, tiles=tiles, tap_tiles=tap_tiles, used=used, whole=whole,
        pad=whole - used, chains=chains, buffers=buffers, most=max(sizes), levels=len(sizes),
    )


def run_block(plan, tokens, upstream, weights, mask):
    count_y, width, hidden = plan.count_y, plan.width, plan.hidden
    lines, length = plan.planes * plan.part_z, plan.part_y * plan.count_y
    count = lines * length
    blocks = (count_y, plan.planes * plan.part_y, plan.part_z * width)
    padded = (plan.planes + 2, plan.part_z + 2, length, width)

    def low(*shape):
        return pltpu.VMEM(shape, LOW)

    def wide(*shape):
        return pltpu.VMEM(shape, WIDE)

    slots = (len(plan.chains), 2 * plan.levels, plan.most)
    scratch = {
        "swap_send": pltpu.SemaphoreType.DMA((4, count_y)),
        "swap_recv": pltpu.SemaphoreType.DMA((4, count_y)),
        "halo_send": pltpu.SemaphoreType.DMA((2, 8)),
        "halo_recv": pltpu.SemaphoreType.DMA((2, 8)),
        "chain_send": pltpu.SemaphoreType.DMA(slots),
        "chain_recv": pltpu.SemaphoreType.DMA(slots),
        "load_sem": pltpu.SemaphoreType.DMA((2 + len(weights),)),
        "leave_sem": pltpu.SemaphoreType.DMA((4,)),
        "qkv_weight": low(width, 3 * width),
        "out_weight": low(width, width),
        "taps": wide(3, 3, 3, width),
        "up_weight": low(width, hidden),
        "down_weight": low(width, hidden),
        "sums": low(plan.whole, 16, 128),
        "token_local": low(*tokens.shape),
        "grad_local": low(*tokens.shape),
        "block_local": low(*tokens.shape),
        "slab": wide(*tokens.shape),
        "token_in": low(*blocks),
        "grad_in": low(*blocks),
        "block_got": low(*blocks),
        "token_back": low(*blocks),
        "token_got": low(*blocks),
        "grad_got": low(*blocks),
        "block_sent": low(*blocks),
        "token_sent": low(*blocks),
        "token_wide": wide(count, width),
        "above_wide": wide(count, width),
        "block_wide": wide(count, width),
        "normal": wide(count, width),
        "inverse": wide(count, 1),
        "query_scale": wide(count, 1),
        "key_scale": wide(count, 1),
        "query_stack": low(lines, HEADS * length, width),
        "key_unit": low(count, width),
        "normal_second": wide(count, width),
        "inverse_second": wide(count, 1),
        "slope": wide(count, hidden),
        "conv_part": wide(count, width),
        "query": low(count, width),
        "key": low(count, width),
        "value": low(count, width),
        "attended": low(count, width),
        "probs": wide(lines, HEADS * length, length),
        "padded_value": low(*padded),
        "padded_grad": low(*padded),
        "mixed": low(count, width),
        "normed": low(count, width),
        "hidden": low(count, hidden),
        "grad_pre": low(count, hidden),
        "tap_sums": wide(27, 8, width),
        "tap_flat": wide(32, 256),
        "grad_value": low(count, width),
        "above": low(count, width),
        "grad_q": low(count, width),
        "grad_k": low(count, width),
        "grad_v": low(count, width),
        "joint": wide(width, 4 * width),
        "parts": wide(plan.whole, 16, 128),
    }
    for name, shape, kind in plan.buffers:
        scratch[name] = pltpu.VMEM(shape, kind)
    names = ["token_slab", "grad_slab", "qkv_hbm", "out_hbm", "taps_hbm", "up_hbm", "down_hbm", "mask"]
    outs = {
        "block_out": jax.ShapeDtypeStruct(tokens.shape, LOW),
        "token_out": jax.ShapeDtypeStruct(tokens.shape, LOW),
        "sums_out": jax.ShapeDtypeStruct((plan.whole, 16, 128), LOW),
    }
    plan.names = names + list(outs) + list(scratch)
    return pl.pallas_call(
        functools.partial(block_kernel, plan),
        out_shape=tuple(outs.values()),
        in_specs=[ANY, ANY] + [ANY] * len(weights) + [SMEM],
        out_specs=(ANY,) * len(outs),
        scratch_shapes=list(scratch.values()),
        compiler_params=pltpu.CompilerParams(
            collective_id=0, has_side_effects=True, vmem_limit_bytes=60 * 1024 * 1024
        ),
        name="block",
    )(tokens, upstream, *weights, mask)


def finish_kernel(plan, factor, sums_in, block_in, token_in, *refs):
    (block_out, token_out, qkv_out, out_out, kernel_out, up_out, down_out) = refs[:7]
    sums, block, token, qkv, out, kernel, up, down, joint, load_sem, sem = refs[7:]
    rows = plan.width // 16
    copies = []

    def leave(source, target):
        copies.append(pltpu.make_async_copy(source, target, sem.at[len(copies)]))
        copies[-1].start()

    def tile(first):
        return sums[first : first + rows].astype(WIDE).reshape(plan.width, 128) * factor

    loads = []
    for source, target in (
        (sums_in.at[: plan.tiles], sums.at[: plan.tiles]),
        (sums_in.at[plan.tiles : 2 * plan.tiles], sums.at[plan.tiles : 2 * plan.tiles]),
        (sums_in.at[2 * plan.tiles :], sums.at[2 * plan.tiles :]),
        (block_in, block),
        (token_in, token),
    ):
        copy = pltpu.make_async_copy(source, target, load_sem.at[len(loads)])
        copy.start()
        loads.append(copy)
    taps_at = 2 * plan.tiles
    joint_at = taps_at + plan.tap_tiles
    for base, target, result, load in (
        (0, up, up_out, loads[0]),
        (plan.tiles, down, down_out, loads[1]),
    ):
        load.wait()
        for index in range(plan.hidden // 128):
            target[:, index * 128 : (index + 1) * 128] = tile(base + index * rows)
        leave(target, result)
    for source, target, load in ((block, block_out, loads[3]), (token, token_out, loads[4])):
        load.wait()
        leave(source, target)
    loads[2].wait()
    for index in range(4 * plan.width // 128):
        joint[:, index * 128 : (index + 1) * 128] = tile(joint_at + index * rows)
    qkv[...] = joint[:, : 3 * plan.width]
    leave(qkv, qkv_out)
    out[...] = joint[:, 3 * plan.width :]
    leave(out, out_out)
    taps = sums[taps_at:joint_at].astype(WIDE) * factor
    flat = jnp.concatenate([taps[:2].reshape(32, 128), taps[2:].reshape(32, 128)], axis=1)
    for a in range(3):
        for b in range(3):
            first = (a * 3 + b) * 3
            kernel[a, b] = flat[first : first + 3, : plan.width]
    leave(kernel, kernel_out)
    for copy in copies:
        copy.wait()


def finish(plan, factor, sums, block_out, token_out):
    width, hidden = plan.width, plan.hidden
    shapes = ((width, 3 * width), (width, width), (3, 3, 3, width), (width, hidden), (width, hidden))
    outs = [jax.ShapeDtypeStruct(block_out.shape, LOW)] * 2
    outs += [jax.ShapeDtypeStruct(shape, WIDE) for shape in shapes]
    return pl.pallas_call(
        functools.partial(finish_kernel, plan, factor),
        out_shape=tuple(outs),
        in_specs=[ANY] * 3,
        out_specs=(ANY,) * len(outs),
        scratch_shapes=[pltpu.VMEM(x.shape, LOW) for x in (sums, block_out, token_out)]
        + [pltpu.VMEM(shape, WIDE) for shape in shapes]
        + [
            pltpu.VMEM((width, 4 * width), WIDE),
            pltpu.SemaphoreType.DMA((5,)),
            pltpu.SemaphoreType.DMA((len(outs),)),
        ],
        compiler_params=pltpu.CompilerParams(vmem_limit_bytes=60 * 1024 * 1024),
        name="finish",
    )(sums, block_out, token_out)


def local(tokens, qkv_weight, out_weight, conv_kernel, up_weight, down_weight, band_mask, grad_out):
    count_y, count_z = lax.axis_size("gy"), lax.axis_size("gz")
    extent_x, part_y, part_z, width = tokens.shape
    planes = extent_x // count_y
    plan = make_plan(count_y, count_z, (planes, part_y, part_z, width), up_weight.shape[1])
    weights = (qkv_weight, out_weight, conv_kernel, up_weight, down_weight.T)
    block_out, token_gradient, sums = run_block(
        plan, tokens, grad_out, weights, band_mask
    )
    factor = 1.0 / math.sqrt(extent_x * part_y * count_y * part_z * count_z)
    block_out, token_gradient, qkv_sum, out_sum, kernel_sum, up_sum, down_sum = finish(
        plan, factor, sums, block_out, token_gradient
    )
    return (
        block_out,
        token_gradient,
        qkv_sum,
        out_sum,
        kernel_sum,
        up_sum,
        down_sum.T,
    )


def solution(mesh):
    placed = (P(None, "gy", "gz", None), P(), P(), P(), P(), P(), P(), P(None, "gy", "gz", None))
    return jax.shard_map(
        local,
        mesh=mesh,
        in_specs=placed,
        out_specs=(P(None, "gy", "gz", None), P(None, "gy", "gz", None), P(), P(), P(), P(), P()),
        check_vma=False,
    )
```

```python
import functools
import math
import types

import jax
import jax.numpy as jnp
from jax import lax
from jax.experimental import pallas as pl
from jax.experimental.pallas import tpu as pltpu
from jax.sharding import PartitionSpec as P

HEADS = 6
BLOCK = 16


NORM_EPS = 1e-05
UNIT_EPS = 1e-06
GELU_SLOPE = 0.7978845608028654
GELU_CUBIC = 0.044715

MESH = pl.DeviceIdType.MESH
SMEM = pl.BlockSpec(memory_space=pltpu.SMEM)
ANY = pl.BlockSpec(memory_space=pl.ANY)
LOW = jnp.bfloat16
WIDE = jnp.float32


def norm_rows(values):
    centred = values - jnp.mean(values, axis=-1, keepdims=True)
    inverse = lax.rsqrt(jnp.mean(centred * centred, axis=-1, keepdims=True) + NORM_EPS)
    return (centred * inverse, inverse)


def norm_rows_back(upstream, normal, inverse):
    return inverse * (
        upstream
        - jnp.mean(upstream, axis=-1, keepdims=True)
        - normal * jnp.mean(upstream * normal, axis=-1, keepdims=True)
    )


def unit_scale(values):
    return lax.rsqrt(jnp.mean(values * values, axis=-1, keepdims=True) + UNIT_EPS)


def unit_back(upstream, values, scaling):
    return scaling * upstream - scaling * scaling * scaling * values * jnp.mean(
        upstream * values, axis=-1, keepdims=True
    )


def place_of(index):
    return index + (1 - 2 * lax.rem(index, 2)) * lax.rem(index // 2, 2)


def dot(left, right, left_axis=1, right_axis=0):
    return lax.dot_general(
        left, right, (((left_axis,), (right_axis,)), ((), ())), preferred_element_type=WIDE
    )


def stack_heads(values):
    width = values.shape[1]
    head_of = lax.broadcasted_iota(jnp.int32, (1, width), 1) // (width // HEADS)
    return jnp.concatenate([jnp.where(head_of == h, values, 0.0) for h in range(HEADS)], axis=0)


def unstack_heads(stacked):
    rows, width = stacked.shape[0] // HEADS, stacked.shape[1]
    head_of = lax.broadcasted_iota(jnp.int32, (1, width), 1) // (width // HEADS)
    joined = stacked[:rows]
    for h in range(1, HEADS):
        joined = jnp.where(head_of == h, stacked[h * rows : (h + 1) * rows], joined)
    return joined


def shift_rows(values, step):
    return pltpu.roll(values, step % values.shape[0], 0)


def face(step, extent):
    return {
        0: (pl.ds(0, extent), pl.ds(1, extent)),
        1: (pl.ds(extent - 1, 1), pl.ds(0, 1)),
        -1: (pl.ds(0, 1), pl.ds(extent + 1, 1)),
    }[step]


def conv_line(padded, taps, plane, column, flip, inside):
    by_shift = [None, None, None]
    for a in range(3):
        for d in range(3):
            x, z = plane + a, column + d
            here = 0 < x < padded.shape[0] - 1 and 0 < z < padded.shape[1] - 1
            if here != inside:
                continue
            window = padded[x, z].astype(WIDE)
            for b in range(3):
                tap = taps[2 - a, 2 - b, 2 - d : 3 - d] if flip else taps[a, b, d : d + 1]
                term = tap * window
                by_shift[b] = term if by_shift[b] is None else by_shift[b] + term
    if by_shift[0] is None:
        return 0.0
    return shift_rows(by_shift[0], 1) + by_shift[1] + shift_rows(by_shift[2], -1)


def put_tiles(target, base, matrix):
    rows = matrix.shape[0] // 16
    for column in range(matrix.shape[1] // 128):
        target[base + column * rows : base + (column + 1) * rows] = matrix[
            :, column * 128 : (column + 1) * 128
        ].reshape(rows, 16, 128)


def spread_mask(mask, length):
    blocks = length // BLOCK
    column = lax.broadcasted_iota(jnp.int32, (BLOCK, length), 1) // BLOCK
    rows = []
    for i in range(blocks):
        row = jnp.zeros((BLOCK, length), jnp.int32)
        for j in range(blocks):
            row = jnp.where(column == j, mask[i, j], row)
        rows.append(row)
    return jnp.concatenate(rows, axis=0).astype(WIDE)


def block_kernel(plan, *refs):
    r = types.SimpleNamespace(**dict(zip(plan.names, refs)))
    count_y, count_z = plan.count_y, plan.count_z
    planes, part_y, part_z, width = plan.planes, plan.part_y, plan.part_z, plan.width
    lines, length = planes * part_z, part_y * count_y
    count = lines * length
    factor = 2.0 / math.sqrt(width // HEADS)
    me_y, me_z = lax.axis_index("gy"), lax.axis_index("gz")
    me_x = place_of(me_y)

    moved = (
        (r.token_slab, r.token_local),
        (r.grad_slab, r.grad_local),
        (r.qkv_hbm, r.qkv_weight),
        (r.out_hbm, r.out_weight),
        (r.taps_hbm, r.taps),
        (r.up_hbm, r.up_weight),
        (r.down_hbm, r.down_weight),
    )
    loads = [
        pltpu.make_async_copy(source, target, r.load_sem.at[index])
        for index, (source, target) in enumerate(moved)
    ]
    for copy in loads:
        copy.start()

    steps = [(-1, 0), (1, 0), (0, -1), (0, 1), (-1, -1), (-1, 1), (1, -1), (1, 1)]
    half_z = max(1, count_z // 2)
    flip = me_y + 1 - 2 * lax.rem(me_y, 2)
    friends = [(lax.rem(me_y + k, count_y), me_z) for k in range(1, count_y)]
    friends += [(me_y, me_z + 1 - 2 * lax.rem(me_z, 2))]
    friends += [
        (peer, lax.rem(me_z + 2 * k, count_z)) for k in range(1, half_z) for peer in (me_y, flip)
    ]
    barrier = pltpu.get_barrier_semaphore()

    def reach(dx, action):
        if dx == 0:
            action()
        elif dx == 1:
            pl.when(me_x < count_y - 1)(action)
        else:
            pl.when(me_x > 0)(action)

    def place(dx, dz):
        return (place_of(me_x + dx), lax.rem(me_z + dz + count_z, count_z))

    def greet(peer):
        pl.semaphore_signal(barrier, inc=1, device_id=peer, device_id_type=MESH)

    for peer in friends:
        greet(peer)
    for dx, dz in steps:
        if dz != 0:
            reach(dx, lambda dx=dx, dz=dz: greet(place(dx, dz)))
    common = len(friends)

    def to_blocks(source, target):
        for p in range(count_y):
            rows = []
            for x in range(p * planes, (p + 1) * planes):
                slab = source[x].astype(WIDE)
                rows.append(jnp.concatenate([slab[:, z] for z in range(part_z)], axis=1))
            target[p] = (rows[0] if planes == 1 else jnp.concatenate(rows, axis=0)).astype(LOW)

    def from_blocks(source, target):
        for p in range(count_y):
            block = source[p].astype(WIDE)
            for i in range(planes):
                x = p * planes + i
                for z in range(part_z):
                    r.slab[x, :, z, :] = block[
                        i * part_y : (i + 1) * part_y, z * width : (z + 1) * width
                    ]
                target[x] = r.slab[x].astype(LOW)

    loads[0].wait()
    to_blocks(r.token_local, r.token_in)
    inner = (me_x > 0) & (me_x < count_y - 1)

    @pl.when(inner)
    def _():
        pl.semaphore_wait(barrier, common + 6)

    @pl.when(jnp.logical_not(inner))
    def _():
        pl.semaphore_wait(barrier, common + 4)

    def swap(source, target, slot, inward, first=1, last=count_y):
        copies = []
        for k in sorted(range(first, last), key=lambda k: abs(2 * k - count_y)):
            peer = lax.rem(me_y + k, count_y)
            copy = pltpu.make_async_remote_copy(
                src_ref=source.at[place_of(peer) if inward else peer],
                dst_ref=target.at[me_y if inward else me_x],
                send_sem=r.swap_send.at[slot, k],
                recv_sem=r.swap_recv.at[slot, k],
                device_id=(peer, me_z),
                device_id_type=MESH,
            )
            copy.start()
            copies.append(copy)
        return copies

    token_copies = swap(r.token_in, r.token_got, 0, True)
    loads[1].wait()
    to_blocks(r.grad_local, r.grad_in)
    grad_copies = swap(r.grad_in, r.grad_got, 1, True, 1, count_y // 2)
    r.token_got[me_y] = r.token_in[me_x]
    r.grad_got[me_y] = r.grad_in[me_x]

    def to_lines(got, target):
        for p in range(count_y):
            block = got[p].astype(WIDE)
            for line in range(lines):
                x, z = line // part_z, line % part_z
                target[pl.ds(line * length + p * part_y, part_y)] = block[
                    x * part_y : (x + 1) * part_y, z * width : (z + 1) * width
                ]

    def from_lines(source, target):
        for p in range(count_y):
            rows = [
                jnp.concatenate(
                    [
                        source[pl.ds((x * part_z + z) * length + p * part_y, part_y)]
                        for z in range(part_z)
                    ],
                    axis=1,
                )
                for x in range(planes)
            ]
            target[p] = (rows[0] if planes == 1 else jnp.concatenate(rows, axis=0)).astype(LOW)

    def conv_inside(padded, flip):
        for line in range(lines):
            plane, column = line // part_z, line % part_z
            r.conv_part[pl.ds(line * length, length)] = padded[plane + 1, column + 1].astype(
                WIDE
            ) + conv_line(padded, r.taps, plane, column, flip, True)

    def conv_rest(padded, line, flip):
        return r.conv_part[pl.ds(line * length, length)] + conv_line(
            padded, r.taps, line // part_z, line % part_z, flip, False
        )

    def halo(padded, slot):
        copies = []
        for index, (dx, dz) in enumerate(steps):
            from_x, to_x = face(dx, planes)
            from_z, to_z = face(dz, part_z)
            inside_x = pl.ds(from_x.start + 1, from_x.size)
            inside_z = pl.ds(from_z.start + 1, from_z.size)
            copies.append(
                lambda index=index, dx=dx, dz=dz, ix=inside_x, iz=inside_z, tx=to_x, tz=to_z: pltpu.make_async_remote_copy(
                    src_ref=padded.at[ix, iz],
                    dst_ref=padded.at[tx, tz],
                    send_sem=r.halo_send.at[slot, index],
                    recv_sem=r.halo_recv.at[slot, index],
                    device_id=place(dx, dz),
                    device_id_type=MESH,
                )
            )
        for index, (dx, dz) in enumerate(steps):
            reach(dx, lambda index=index: copies[index]().start())
        blank = jnp.zeros((1,) + tuple(padded.shape[1:]), padded.dtype)

        @pl.when(me_x == 0)
        def _():
            padded[0:1] = blank

        @pl.when(me_x == count_y - 1)
        def _():
            padded[planes + 1 : planes + 2] = blank

        def finish():
            for index, (dx, dz) in enumerate(steps):
                reach(dx, lambda index=index: copies[index]().wait_send())
                reach(-dx, lambda index=index: copies[index]().wait_recv())

        return finish

    me_core, me_chip = lax.rem(me_z, 2), me_z // 2

    me_even, me_far = lax.rem(me_y, 2), me_y // 2
    far = count_y // 2

    def sibling(k):
        peer = lax.rem(me_core + k, 2)
        return peer, (me_y, me_chip * 2 + peer)

    def near(k):
        even = lax.rem(me_even + k // half_z, 2)
        chip = lax.rem(me_chip + k % half_z, half_z)
        return even * half_z + chip, (me_far * 2 + even, chip * 2 + me_core)

    def distant(k):
        peer = lax.rem(me_far + k, far)
        return peer, (peer * 2 + me_even, me_z)

    groups = (
        (2, me_core, sibling),
        (2 * half_z, me_even * half_z + me_chip, near),
        (far, me_far, distant),
    )

    def send(source, target, chain, stage, k, peer):
        copy = pltpu.make_async_remote_copy(
            src_ref=source,
            dst_ref=target,
            send_sem=r.chain_send.at[chain, stage, k],
            recv_sem=r.chain_recv.at[chain, stage, k],
            device_id=peer,
            device_id_type=MESH,
        )
        copy.start()
        return copy

    def run_chain(chain):
        entry = plan.chains[chain]
        sums = r.sums
        base, size = entry.base, entry.size
        held, first = r.parts, base
        spans = []
        for level, (total, me, peer_of) in enumerate(groups):
            outgoing, incoming, result = (getattr(r, name) for name in entry.buffers[level])
            part = size // total
            outgoing[...] = held[pl.ds(first, size)].astype(LOW)
            copies = []
            for k in range(1, total):
                index, peer = peer_of(k)
                copies.append(
                    send(
                        outgoing.at[pl.ds(index * part, part)], incoming.at[k], chain, level, k, peer
                    )
                )
            yield
            summed = held[pl.ds(first + me * part, part)]
            for k, copy in enumerate(copies):
                copy.wait()
                summed = summed + incoming[k + 1].astype(WIDE)
            result[...] = summed
            held, first = result, 0
            base, size = base + me * part, part
            spans.append((base, size))
        sums[pl.ds(base, size)] = held[...].astype(LOW)
        for level in range(len(groups) - 1, -1, -1):
            total, _, peer_of = groups[level]
            span = pl.ds(*spans[level])
            copies = [
                send(sums.at[span], sums.at[span], chain, len(groups) + level, k, peer_of(k)[1])
                for k in range(1, total)
            ]
            yield
            for copy in copies:
                copy.wait()

    def leave(source, target, slot):
        copy = pltpu.make_async_copy(source, target, r.leave_sem.at[slot])
        copy.start()
        return copy

    running = []

    def launch(chain):
        if plan.chains[chain]:
            running.append(run_chain(chain))
            next(running[-1])

    def advance():
        for work in list(reversed(running)):
            if next(work, "done") == "done":
                running.remove(work)

    mask = jnp.tile(spread_mask(r.mask, length), (HEADS, 1))
    for copy in loads[2:]:
        copy.wait()
    for copy in token_copies:
        copy.wait()
    to_lines(r.token_got, r.token_wide)
    token_wide = r.token_wide[...]
    normal, inverse = norm_rows(token_wide)
    r.normal[...] = normal
    r.inverse[...] = inverse
    normed = normal.astype(LOW)
    for piece, target in enumerate((r.query, r.key, r.value)):
        target[...] = dot(normed, r.qkv_weight[:, piece * width : (piece + 1) * width]).astype(LOW)
    for line in range(lines):
        rows = pl.ds(line * length, length)
        query_vec, key_vec = r.query[rows].astype(WIDE), r.key[rows].astype(WIDE)
        query_stack = stack_heads(query_vec * unit_scale(query_vec)).astype(LOW)
        key_unit = (key_vec * unit_scale(key_vec)).astype(LOW)
        weights = mask * jnp.exp(factor * dot(query_stack, key_unit, 1, 1))
        probs = weights / jnp.sum(weights, axis=-1, keepdims=True)
        r.probs[line] = probs
        r.attended[rows] = unstack_heads(dot(probs.astype(LOW), r.value[rows])).astype(LOW)
    field = (r.token_wide[...] + dot(r.attended[...], r.out_weight[...])).astype(LOW)
    r.padded_value[1 : planes + 1, 1 : part_z + 1] = field.reshape(planes, part_z, length, width)
    finish_value = halo(r.padded_value, 0)
    grad_copies += swap(r.grad_in, r.grad_got, 1, True, count_y // 2)

    conv_inside(r.padded_value, False)
    finish_value()
    for line in range(lines):
        r.mixed[pl.ds(line * length, length)] = conv_rest(r.padded_value, line, False).astype(LOW)
    group = min(2, part_z)
    for start in range(0, lines, group):
        rows = pl.ds(start * length, group * length)
        mixed_wide = r.mixed[rows].astype(WIDE)
        normal, inverse = norm_rows(mixed_wide)
        r.normal_second[rows] = normal
        r.inverse_second[rows] = inverse
        r.normed[rows] = normal.astype(LOW)
        pre_act = dot(r.normed[rows], r.up_weight[...])
        square = pre_act * pre_act
        tangent = jnp.tanh(GELU_SLOPE * (pre_act + GELU_CUBIC * square * pre_act))
        r.hidden[rows] = (0.5 * pre_act * (1.0 + tangent)).astype(LOW)
        r.slope[rows] = 0.5 * (1.0 + tangent) + 0.5 * pre_act * (
            1.0 - tangent * tangent
        ) * GELU_SLOPE * (1.0 + 3.0 * GELU_CUBIC * square)
        r.block_wide[rows] = mixed_wide + dot(r.hidden[rows], r.down_weight[...], 1, 1)

    for copy in grad_copies:
        copy.wait()
    to_lines(r.grad_got, r.above_wide)
    for start in range(0, lines, group):
        plane, columns = start // part_z, pl.ds(start % part_z + 1, group)
        rows = pl.ds(start * length, group * length)
        grad_hidden = dot(r.above_wide[rows].astype(LOW), r.down_weight[...]).astype(LOW)
        r.grad_pre[rows] = (grad_hidden.astype(WIDE) * r.slope[rows]).astype(LOW)
        grad_normed = dot(r.grad_pre[rows], r.up_weight[...], 1, 1)
        r.padded_grad[plane + 1, columns] = (
            (
                r.above_wide[rows]
                + norm_rows_back(grad_normed, r.normal_second[rows], r.inverse_second[rows])
            )
            .astype(LOW)
            .reshape(group, length, width)
        )
    finish_grad = halo(r.padded_grad, 1)
    put_tiles(r.parts, 0, dot(r.normed[...], r.grad_pre[...], 0, 0))
    put_tiles(r.parts, plan.tiles, dot(r.above_wide[...].astype(LOW), r.hidden[...], 0, 0))
    launch(0)

    r.tap_sums[...] = jnp.zeros_like(r.tap_sums)
    for line in range(lines):
        plane, column = line // part_z, line % part_z
        centre = r.padded_grad[plane + 1, column + 1].astype(WIDE)
        shifted = (shift_rows(centre, -1), centre, shift_rows(centre, 1))
        for a in range(3):
            for d in range(3):
                window = r.padded_value[plane + a, column + d].astype(WIDE)
                for b in range(3):
                    product = (shifted[b] * window).reshape(length // 8, 8, width)
                    r.tap_sums[(a * 3 + b) * 3 + d] += jnp.sum(product, axis=0)
    r.tap_flat[...] = jnp.zeros_like(r.tap_flat)
    r.tap_flat[:27, :width] = jnp.sum(r.tap_sums[...], axis=1)
    put_tiles(r.parts, 2 * plan.tiles, r.tap_flat[...])
    if plan.pad:
        r.parts[plan.used :] = jnp.zeros((plan.pad, 16, 128), WIDE)
    from_lines(r.block_wide, r.block_sent)
    conv_inside(r.padded_grad, True)
    advance()
    finish_grad()
    block_copies = swap(r.block_sent, r.block_got, 2, False)
    r.block_got[me_x] = r.block_sent[me_y]

    for line in range(lines):
        r.grad_value[pl.ds(line * length, length)] = conv_rest(r.padded_grad, line, True).astype(LOW)
    r.above[...] = dot(r.grad_value[...], r.out_weight[...], 1, 1).astype(LOW)
    r.joint[:, 3 * width :] = dot(r.attended[...], r.grad_value[...], 0, 0)
    for line in range(lines):
        rows = pl.ds(line * length, length)
        query_vec, key_vec = r.query[rows].astype(WIDE), r.key[rows].astype(WIDE)
        query_scale, key_scale = unit_scale(query_vec), unit_scale(key_vec)
        query_stack = stack_heads(query_vec * query_scale).astype(LOW)
        key_unit = (key_vec * key_scale).astype(LOW)
        probs = r.probs[line]
        grad_stack = stack_heads(r.above[rows].astype(WIDE)).astype(LOW)
        grad_probs = dot(grad_stack, r.value[rows], 1, 1)
        grad_scores = probs * (grad_probs - jnp.sum(grad_probs * probs, axis=-1, keepdims=True))
        grad_low = (factor * grad_scores).astype(LOW)
        r.grad_v[rows] = dot(probs.astype(LOW), grad_stack, 0, 0).astype(LOW)
        grad_qunit = unstack_heads(dot(grad_low, key_unit))
        grad_kunit = dot(grad_low, query_stack, 0, 0)
        r.grad_q[rows] = unit_back(grad_qunit, query_vec, query_scale).astype(LOW)
        r.grad_k[rows] = unit_back(grad_kunit, key_vec, key_scale).astype(LOW)
    advance()
    normal = r.normal[...]
    normed = normal.astype(LOW)
    pieces = [
        (slice(piece * width, (piece + 1) * width), grad)
        for piece, grad in enumerate((r.grad_q, r.grad_k, r.grad_v))
    ]
    for part, grad in pieces:
        r.joint[:, part] = dot(normed, grad[...], 0, 0)
    put_tiles(r.parts, 2 * plan.tiles + plan.tap_tiles, r.joint[...])
    launch(1)
    grad_normed = 0.0
    for part, grad in pieces:
        grad_normed = grad_normed + dot(grad[...], r.qkv_weight[:, part], 1, 1)
    upstream = grad_normed.astype(LOW).astype(WIDE)
    r.block_wide[...] = r.grad_value[...].astype(WIDE) + norm_rows_back(
        upstream, normal, r.inverse[...]
    )
    from_lines(r.block_wide, r.token_sent)
    token_copies = swap(r.token_sent, r.token_back, 3, False)
    r.token_back[me_x] = r.token_sent[me_y]
    advance()
    for copy in block_copies:
        copy.wait()
    from_blocks(r.block_got, r.block_local)
    leaves = [leave(r.block_local, r.block_out, 0)]
    advance()
    advance()
    for copy in token_copies:
        copy.wait()
    from_blocks(r.token_back, r.token_local)
    leaves.append(leave(r.token_local, r.token_out, 1))
    while len(running) > 1:
        advance()
    cut = plan.chains[1].base
    if cut:
        leaves.append(leave(r.sums.at[:cut], r.sums_out.at[:cut], 2))
    while running:
        advance()
    leaves.append(leave(r.sums.at[cut:], r.sums_out.at[cut:], 3))
    for copy in leaves:
        copy.wait()


def make_plan(count_y, count_z, extents, hidden_width):
    planes, part_y, part_z, width = extents
    devices = count_y * count_z
    rows = width // 16
    tiles = rows * (hidden_width // 128)
    tap_tiles = 4
    used = 2 * tiles + tap_tiles + rows * (4 * width // 128)
    whole = -(-used // devices) * devices
    chains, buffers = [], []
    cut = 2 * tiles // devices * devices
    sizes = (2, count_z // 2 * 2, count_y // 2)
    for index, (base, size) in enumerate(((0, cut), (cut, whole - cut))):
        names, left = [], size
        for level, total in enumerate(sizes):
            part = left // total
            names.append(["chain%d_%s%d" % (index, kind, level) for kind in ("out", "in", "sum")])
            shapes = ((left, 16, 128), (total, part, 16, 128), (part, 16, 128))
            buffers += list(zip(names[-1], shapes, (LOW, LOW, WIDE))) if size else []
            left = part
        chains.append(types.SimpleNamespace(base=base, size=size, buffers=names) if size else None)
    return types.SimpleNamespace(
        count_y=count_y, count_z=count_z, planes=planes, part_y=part_y, part_z=part_z, width=width,
        hidden=hidden_width, tiles=tiles, tap_tiles=tap_tiles, used=used, whole=whole,
        pad=whole - used, chains=chains, buffers=buffers, most=max(sizes), levels=len(sizes),
    )


def run_block(plan, tokens, upstream, weights, mask):
    count_y, width, hidden = plan.count_y, plan.width, plan.hidden
    lines, length = plan.planes * plan.part_z, plan.part_y * plan.count_y
    count = lines * length
    blocks = (count_y, plan.planes * plan.part_y, plan.part_z * width)
    padded = (plan.planes + 2, plan.part_z + 2, length, width)

    def low(*shape):
        return pltpu.VMEM(shape, LOW)

    def wide(*shape):
        return pltpu.VMEM(shape, WIDE)

    slots = (len(plan.chains), 2 * plan.levels, plan.most)
    scratch = {
        "swap_send": pltpu.SemaphoreType.DMA((4, count_y)),
        "swap_recv": pltpu.SemaphoreType.DMA((4, count_y)),
        "halo_send": pltpu.SemaphoreType.DMA((2, 8)),
        "halo_recv": pltpu.SemaphoreType.DMA((2, 8)),
        "chain_send": pltpu.SemaphoreType.DMA(slots),
        "chain_recv": pltpu.SemaphoreType.DMA(slots),
        "load_sem": pltpu.SemaphoreType.DMA((2 + len(weights),)),
        "leave_sem": pltpu.SemaphoreType.DMA((4,)),
        "qkv_weight": low(width, 3 * width),
        "out_weight": low(width, width),
        "taps": wide(3, 3, 3, width),
        "up_weight": low(width, hidden),
        "down_weight": low(width, hidden),
        "sums": low(plan.whole, 16, 128),
        "token_local": low(*tokens.shape),
        "grad_local": low(*tokens.shape),
        "block_local": low(*tokens.shape),
        "slab": wide(*tokens.shape),
        "token_in": low(*blocks),
        "grad_in": low(*blocks),
        "block_got": low(*blocks),
        "token_back": low(*blocks),
        "token_got": low(*blocks),
        "grad_got": low(*blocks),
        "block_sent": low(*blocks),
        "token_sent": low(*blocks),
        "token_wide": wide(count, width),
        "above_wide": wide(count, width),
        "block_wide": wide(count, width),
        "normal": wide(count, width),
        "inverse": wide(count, 1),
        "normal_second": wide(count, width),
        "inverse_second": wide(count, 1),
        "slope": wide(count, hidden),
        "conv_part": wide(count, width),
        "query": low(count, width),
        "key": low(count, width),
        "value": low(count, width),
        "attended": low(count, width),
        "probs": wide(lines, HEADS * length, length),
        "padded_value": low(*padded),
        "padded_grad": low(*padded),
        "mixed": low(count, width),
        "normed": low(count, width),
        "hidden": low(count, hidden),
        "grad_pre": low(count, hidden),
        "tap_sums": wide(27, 8, width),
        "tap_flat": wide(32, 256),
        "grad_value": low(count, width),
        "above": low(count, width),
        "grad_q": low(count, width),
        "grad_k": low(count, width),
        "grad_v": low(count, width),
        "joint": wide(width, 4 * width),
        "parts": wide(plan.whole, 16, 128),
    }
    for name, shape, kind in plan.buffers:
        scratch[name] = pltpu.VMEM(shape, kind)
    names = ["token_slab", "grad_slab", "qkv_hbm", "out_hbm", "taps_hbm", "up_hbm", "down_hbm", "mask"]
    outs = {
        "block_out": jax.ShapeDtypeStruct(tokens.shape, LOW),
        "token_out": jax.ShapeDtypeStruct(tokens.shape, LOW),
        "sums_out": jax.ShapeDtypeStruct((plan.whole, 16, 128), LOW),
    }
    plan.names = names + list(outs) + list(scratch)
    return pl.pallas_call(
        functools.partial(block_kernel, plan),
        out_shape=tuple(outs.values()),
        in_specs=[ANY, ANY] + [ANY] * len(weights) + [SMEM],
        out_specs=(ANY,) * len(outs),
        scratch_shapes=list(scratch.values()),
        compiler_params=pltpu.CompilerParams(
            collective_id=0, has_side_effects=True, vmem_limit_bytes=60 * 1024 * 1024
        ),
        name="block",
    )(tokens, upstream, *weights, mask)


def finish_kernel(plan, factor, sums_in, block_in, token_in, *refs):
    (block_out, token_out, qkv_out, out_out, kernel_out, up_out, down_out) = refs[:7]
    sums, block, token, qkv, out, kernel, up, down, joint, load_sem, sem = refs[7:]
    rows = plan.width // 16
    copies = []

    def leave(source, target):
        copies.append(pltpu.make_async_copy(source, target, sem.at[len(copies)]))
        copies[-1].start()

    def tile(first):
        return sums[first : first + rows].astype(WIDE).reshape(plan.width, 128) * factor

    loads = []
    for source, target in (
        (sums_in.at[: plan.tiles], sums.at[: plan.tiles]),
        (sums_in.at[plan.tiles : 2 * plan.tiles], sums.at[plan.tiles : 2 * plan.tiles]),
        (sums_in.at[2 * plan.tiles :], sums.at[2 * plan.tiles :]),
        (block_in, block),
        (token_in, token),
    ):
        copy = pltpu.make_async_copy(source, target, load_sem.at[len(loads)])
        copy.start()
        loads.append(copy)
    taps_at = 2 * plan.tiles
    joint_at = taps_at + plan.tap_tiles
    for base, target, result, load in (
        (0, up, up_out, loads[0]),
        (plan.tiles, down, down_out, loads[1]),
    ):
        load.wait()
        for index in range(plan.hidden // 128):
            target[:, index * 128 : (index + 1) * 128] = tile(base + index * rows)
        leave(target, result)
    for source, target, load in ((block, block_out, loads[3]), (token, token_out, loads[4])):
        load.wait()
        leave(source, target)
    loads[2].wait()
    for index in range(4 * plan.width // 128):
        joint[:, index * 128 : (index + 1) * 128] = tile(joint_at + index * rows)
    qkv[...] = joint[:, : 3 * plan.width]
    leave(qkv, qkv_out)
    out[...] = joint[:, 3 * plan.width :]
    leave(out, out_out)
    taps = sums[taps_at:joint_at].astype(WIDE) * factor
    flat = jnp.concatenate([taps[:2].reshape(32, 128), taps[2:].reshape(32, 128)], axis=1)
    for a in range(3):
        for b in range(3):
            first = (a * 3 + b) * 3
            kernel[a, b] = flat[first : first + 3, : plan.width]
    leave(kernel, kernel_out)
    for copy in copies:
        copy.wait()


def finish(plan, factor, sums, block_out, token_out):
    width, hidden = plan.width, plan.hidden
    shapes = ((width, 3 * width), (width, width), (3, 3, 3, width), (width, hidden), (width, hidden))
    outs = [jax.ShapeDtypeStruct(block_out.shape, LOW)] * 2
    outs += [jax.ShapeDtypeStruct(shape, WIDE) for shape in shapes]
    return pl.pallas_call(
        functools.partial(finish_kernel, plan, factor),
        out_shape=tuple(outs),
        in_specs=[ANY] * 3,
        out_specs=(ANY,) * len(outs),
        scratch_shapes=[pltpu.VMEM(x.shape, LOW) for x in (sums, block_out, token_out)]
        + [pltpu.VMEM(shape, WIDE) for shape in shapes]
        + [
            pltpu.VMEM((width, 4 * width), WIDE),
            pltpu.SemaphoreType.DMA((5,)),
            pltpu.SemaphoreType.DMA((len(outs),)),
        ],
        compiler_params=pltpu.CompilerParams(vmem_limit_bytes=60 * 1024 * 1024),
        name="finish",
    )(sums, block_out, token_out)


def local(tokens, qkv_weight, out_weight, conv_kernel, up_weight, down_weight, band_mask, grad_out):
    count_y, count_z = lax.axis_size("gy"), lax.axis_size("gz")
    extent_x, part_y, part_z, width = tokens.shape
    planes = extent_x // count_y
    plan = make_plan(count_y, count_z, (planes, part_y, part_z, width), up_weight.shape[1])
    weights = (qkv_weight, out_weight, conv_kernel, up_weight, down_weight.T)
    block_out, token_gradient, sums = run_block(
        plan, tokens, grad_out, weights, band_mask
    )
    factor = 1.0 / math.sqrt(extent_x * part_y * count_y * part_z * count_z)
    block_out, token_gradient, qkv_sum, out_sum, kernel_sum, up_sum, down_sum = finish(
        plan, factor, sums, block_out, token_gradient
    )
    return (
        block_out,
        token_gradient,
        qkv_sum,
        out_sum,
        kernel_sum,
        up_sum,
        down_sum.T,
    )


def solution(mesh):
    placed = (P(None, "gy", "gz", None), P(), P(), P(), P(), P(), P(), P(None, "gy", "gz", None))
    return jax.shard_map(
        local,
        mesh=mesh,
        in_specs=placed,
        out_specs=(P(None, "gy", "gz", None), P(None, "gy", "gz", None), P(), P(), P(), P(), P()),
        check_vma=False,
    )
```
